32 devices in a mesh: dp: 8 (over z, y), shard: 4 (over x, core).
Axes of the slice: x: 2, y: 2, z: 4, core: 2. Of those that a mesh axis runs over, the one named last changes fastest.
Arguments:
- tokens_in: bfloat16 [4096, 1088], P(('dp', 'shard')), may hold values from -6 to 6
- cotangent: bfloat16 [4096, 1088], P(('dp', 'shard')), may hold values from -6 to 6
- segment_ids: int32 [4096], P('dp'), may hold values from -1 to 3, as said below
- w_qkv: float32 [1088, 3264], P('shard', 'dp'), may hold values from -0.1875 to 0.1875
- w_attn_out: float32 [1088, 1088], P('shard', 'dp'), may hold values from -0.75 to 0.75
- w_fc: float32 [1088, 4352], P('shard', 'dp'), may hold values from -0.1875 to 0.1875
- w_proj: float32 [4352, 1088], P('shard', 'dp'), may hold values from -0.09375 to 0.09375
- small_w: float32 [12, 1088], P(None, 'shard'), may hold values from -0.8 to 1.8
- moment_qkv: float32 [1088, 3264], P('shard', 'dp'), may hold values from -8 to 8
- moment_attn_out: float32 [1088, 1088], P('shard', 'dp'), may hold values from -8 to 8
- moment_fc: float32 [1088, 4352], P('shard', 'dp'), may hold values from -8 to 8
- moment_proj: float32 [4352, 1088], P('shard', 'dp'), may hold values from -8 to 8
- moment_small: float32 [12, 1088], P(None, 'shard'), may hold values from -8 to 8
- second_qkv: float32 [1088, 3264], P('shard', 'dp'), may hold values from 128 to 512
- second_attn_out: float32 [1088, 1088], P('shard', 'dp'), may hold values from 128 to 512
- second_fc: float32 [1088, 4352], P('shard', 'dp'), may hold values from 128 to 512
- second_proj: float32 [4352, 1088], P('shard', 'dp'), may hold values from 128 to 512
- second_small: float32 [12, 1088], P(None, 'shard'), may hold values from 128 to 512
Outputs:
- out_act: bfloat16 [4096, 1088], P(('dp', 'shard'))
- grad_input: bfloat16 [4096, 1088], P(('dp', 'shard'))
- grad_qkv: float32 [1088, 3264], P('shard', 'dp')
- grad_attn_out: float32 [1088, 1088], P('shard', 'dp')
- grad_fc: float32 [1088, 4352], P('shard', 'dp')
- grad_proj: float32 [4352, 1088], P('shard', 'dp')
- grad_small: float32 [12, 1088], P(None, 'shard')
- new_qkv: float32 [1088, 3264], P('shard', 'dp')
- new_attn_out: float32 [1088, 1088], P('shard', 'dp')
- new_fc: float32 [1088, 4352], P('shard', 'dp')
- new_proj: float32 [4352, 1088], P('shard', 'dp')
- new_small: float32 [12, 1088], P(None, 'shard')
- new_moment_qkv: float32 [1088, 3264], P('shard', 'dp')
- new_moment_attn_out: float32 [1088, 1088], P('shard', 'dp')
- new_moment_fc: float32 [1088, 4352], P('shard', 'dp')
- new_moment_proj: float32 [4352, 1088], P('shard', 'dp')
- new_moment_small: float32 [12, 1088], P(None, 'shard')
- new_second_qkv: float32 [1088, 3264], P('shard', 'dp')
- new_second_attn_out: float32 [1088, 1088], P('shard', 'dp')
- new_second_fc: float32 [1088, 4352], P('shard', 'dp')
- new_second_proj: float32 [4352, 1088], P('shard', 'dp')
- new_second_small: float32 [12, 1088], P(None, 'shard')
The draws below stay inside these ranges and needn't reach their ends.
Inputs may be any that keep to these rules, and one draw needn't show every extreme that they name: `segment_ids`: within each group of 512 consecutive slots the ids number that group's sequences 0, 1, 2, ... in order and the group's first slot has id 0; each sequence begins at a multiple of 128, spans at most 4 blocks and ends inside its last block; -1 marks padding slots after a sequence's end. In the first group every block starts a sequence.
All inputs are finite; a program needn't handle non-finite values.
Results may differ from the reference program's by a relative error of at most 0.022.
Values may be sent and summed in bfloat16 or wider, within the bound.
A program may use at most 192 MiB of HBM per device.

```python
import math
import jax
import jax.numpy as jnp
from jax import lax

D = 1088
H = 17
HD = 64
FF = 4352
TOK_DEV = 128
BLOCK = 128
STEP = 3
GROUP = 512
TOKENS = 4096
N_DP = 8
N_SHARD = 4


def draw_segment_ids(key, part):
    block_count = GROUP // BLOCK
    group_count = TOKENS // GROUP
    key_used, key_start, key_tail = jax.random.split(key, 3)
    used_blocks = jax.random.randint(key_used, (group_count,), block_count // 2, block_count + 1)
    start_bits = jax.random.randint(key_start, (group_count, block_count), 0, 2)
    tail_pads = jax.random.randint(key_tail, (group_count, block_count), 0, BLOCK // 2)
    group_index = jnp.arange(group_count, dtype=jnp.int32)
    used_blocks = jnp.where(group_index == 0, block_count, used_blocks).astype(jnp.int32)
    start_bits = jnp.where(group_index[:, None] == 0, 1, start_bits).astype(jnp.int32)
    block_index = jnp.arange(block_count, dtype=jnp.int32)
    token_index = jnp.arange(BLOCK, dtype=jnp.int32)

    def one_group(used_count, start_row, tail_row):

        def advance(carry, inputs):
            run_length, segment = carry
            position, start_bit = inputs
            begins = (position == 0) | (start_bit == 1) | (run_length >= 4)
            segment = jnp.where(begins, segment + 1, segment).astype(jnp.int32)
            run_length = jnp.where(begins, 1, run_length + 1).astype(jnp.int32)
            return ((run_length, segment), segment)
        final_state, block_segment = lax.scan(advance, (jnp.int32(0), jnp.int32(-1)), (block_index, start_row))
        ends_next = jnp.concatenate([block_segment[1:] != block_segment[:-1], jnp.array([True])])
        last_block = ends_next | (block_index == used_count - 1)
        block_ids = jnp.where(block_index < used_count, block_segment, -1)
        padded = last_block[:, None] & (token_index[None, :] >= BLOCK - tail_row[:, None])
        return jnp.where(padded, -1, block_ids[:, None]).reshape(GROUP)
    return jax.vmap(one_group)(used_blocks, start_bits, tail_pads).reshape(TOKENS).astype(jnp.int32)


def draw_small_w(key, part):
    noise_draw = jnp.clip(jax.random.normal(key, (12, D), jnp.float32), -4.0, 4.0) * 0.2
    row_index = jnp.arange(12)
    gain_rows = (row_index == 0) | (row_index == 5)
    return jnp.where(gain_rows[:, None], 1.0 + noise_draw, noise_draw)


def steps_of(rng, extent, cuts, least, high):
    loudness, own = 1.0, jax.random.fold_in(rng, 6)
    for dim, blocks in cuts:
        steps = jnp.exp(jax.random.uniform(jax.random.fold_in(own, dim), (blocks,), jnp.float32, least / len(cuts), high / len(cuts)))
        loudness = loudness * jnp.repeat(steps, extent[dim] // blocks).reshape([-1 if axis == dim else 1 for axis in range(len(extent))])
    return loudness


def centred(rng, shape, scale, reach, pieces=(), kind=jnp.bfloat16):
    loudness = steps_of(rng, shape, pieces, -0.22, 0.18) if pieces else 1.0
    values = jax.random.normal(rng, shape, jnp.float32) * scale * loudness
    return jnp.minimum(jnp.maximum(values, -reach), reach).astype(kind)


def setup_inputs(seed: int = 0) -> dict:
    seeds = jax.random.split(jax.random.key(seed), 19)
    tokens_in = centred(seeds[0], (TOKENS, D), 1.0, 6.0, ((0, 32),))
    cotangent = centred(seeds[1], (TOKENS, D), 1.0, 6.0, ((0, 32),))
    segment_ids = draw_segment_ids(jax.random.fold_in(seeds[18], 71), 0)
    w_qkv = centred(seeds[3], (D, 3 * D), D ** -0.5, 0.1875, ((0, 4), (1, 8)), jnp.float32)
    w_attn_out = centred(seeds[4], (D, D), (D // 16) ** -0.5, 0.75, ((0, 4), (1, 8)), jnp.float32)
    w_fc = centred(seeds[5], (D, FF), D ** -0.5, 0.1875, ((0, 4), (1, 8)), jnp.float32)
    w_proj = centred(seeds[6], (FF, D), FF ** -0.5, 0.09375, ((0, 4), (1, 8)), jnp.float32)
    small_w = draw_small_w(jax.random.fold_in(seeds[18], 71), 0)
    moment_qkv = jnp.clip(jax.random.uniform(seeds[8], (D, 3 * D), jnp.float32, -8.0, 8.0) * steps_of(seeds[8], (D, 3 * D), ((0, 4), (1, 8)), -0.4, 0.0), -8.0, 8.0)
    moment_attn_out = jnp.clip(jax.random.uniform(seeds[9], (D, D), jnp.float32, -8.0, 8.0) * steps_of(seeds[9], (D, D), ((0, 4), (1, 8)), -0.4, 0.0), -8.0, 8.0)
    moment_fc = jnp.clip(jax.random.uniform(seeds[10], (D, FF), jnp.float32, -8.0, 8.0) * steps_of(seeds[10], (D, FF), ((0, 4), (1, 8)), -0.4, 0.0), -8.0, 8.0)
    moment_proj = jnp.clip(jax.random.uniform(seeds[11], (FF, D), jnp.float32, -8.0, 8.0) * steps_of(seeds[11], (FF, D), ((0, 4), (1, 8)), -0.4, 0.0), -8.0, 8.0)
    moment_small = jnp.clip(jax.random.uniform(seeds[12], (12, D), jnp.float32, -8.0, 8.0) * steps_of(seeds[12], (12, D), ((1, 4),), -0.4, 0.0), -8.0, 8.0)
    second_qkv = jnp.clip(jnp.exp(math.log(512.0) - 1.3862944 * jax.random.uniform(seeds[13], (D, 3 * D), jnp.float32) ** steps_of(seeds[13], (D, 3 * D), ((0, 4), (1, 8)), -0.2, 0.2)), 128.0, 512.0)
    second_attn_out = jnp.clip(jnp.exp(math.log(512.0) - 1.3862944 * jax.random.uniform(seeds[14], (D, D), jnp.float32) ** steps_of(seeds[14], (D, D), ((0, 4), (1, 8)), -0.2, 0.2)), 128.0, 512.0)
    second_fc = jnp.clip(jnp.exp(math.log(512.0) - 1.3862944 * jax.random.uniform(seeds[15], (D, FF), jnp.float32) ** steps_of(seeds[15], (D, FF), ((0, 4), (1, 8)), -0.2, 0.2)), 128.0, 512.0)
    second_proj = jnp.clip(jnp.exp(math.log(512.0) - 1.3862944 * jax.random.uniform(seeds[16], (FF, D), jnp.float32) ** steps_of(seeds[16], (FF, D), ((0, 4), (1, 8)), -0.2, 0.2)), 128.0, 512.0)
    second_small = jnp.clip(jnp.exp(math.log(512.0) - 1.3862944 * jax.random.uniform(seeds[17], (12, D), jnp.float32) ** steps_of(seeds[17], (12, D), ((1, 4),), -0.2, 0.2)), 128.0, 512.0)
    return dict(tokens_in=tokens_in, cotangent=cotangent, segment_ids=segment_ids, w_qkv=w_qkv, w_attn_out=w_attn_out, w_fc=w_fc, w_proj=w_proj, small_w=small_w, moment_qkv=moment_qkv, moment_attn_out=moment_attn_out, moment_fc=moment_fc, moment_proj=moment_proj, moment_small=moment_small, second_qkv=second_qkv, second_attn_out=second_attn_out, second_fc=second_fc, second_proj=second_proj, second_small=second_small)


NORM_EPS = 1e-05
LEARN_RATE = 0.01
BETA_ONE = 0.9
BETA_TWO = 0.95
ADAM_EPS = 1e-08
WEIGHT_DECAY = 0.1

def round_trip(array_in):
    return lax.optimization_barrier(array_in.astype(jnp.bfloat16)).astype(jnp.float32)

def to_float(array_in):
    return array_in.astype(jnp.float32)

def matmul(left_rows, right_rows):
    return jnp.dot(left_rows, right_rows, preferred_element_type=jnp.float32)

def back_product(left_rows, right_rows):
    return jnp.dot(left_rows, right_rows.T, preferred_element_type=jnp.float32)

def norm_forward(row_data, gain_row, shift_row):
    row_mean = lax.optimization_barrier(jnp.mean(row_data, axis=-1, keepdims=True))
    centered = row_data - row_mean
    variance = lax.optimization_barrier(jnp.mean(centered * centered, axis=-1, keepdims=True))
    inverse_dev = lax.rsqrt(variance + NORM_EPS)
    normed = centered * inverse_dev
    return (normed, inverse_dev, normed * gain_row + shift_row)

def norm_backward(grad_rows, normed, inverse_dev, gain_row):
    scaled = grad_rows * gain_row
    return inverse_dev * (scaled - lax.optimization_barrier(jnp.mean(scaled, axis=-1, keepdims=True)) - normed * lax.optimization_barrier(jnp.mean(scaled * normed, axis=-1, keepdims=True)))

def gelu_slope(pre_act):
    normal_cdf = 0.5 * (1.0 + lax.erf(pre_act * 0.7071067811865476))
    normal_pdf = jnp.exp(-0.5 * pre_act * pre_act) * 0.3989422804014327
    return normal_cdf + pre_act * normal_pdf

def head_split(rows_in):
    return to_float(rows_in).reshape(rows_in.shape[0], H, HD)

def prob_table(queries, key_rows, allowed, log_total):
    score_scale = 1.0 / math.sqrt(HD)
    scores = jnp.einsum('rhe,khe->hrk', head_split(queries), head_split(key_rows)) * score_scale
    if log_total is None:
        exp_scores = jnp.where(allowed[None], jnp.exp(scores), 0.0)
        log_total = jnp.log(lax.optimization_barrier(jnp.sum(exp_scores, axis=-1)))
    prob_full = jnp.where(allowed[None], jnp.exp(scores - log_total[..., None]), 0.0)
    return (prob_full, log_total)

def attend_forward(queries, key_rows, value_rows, allowed):
    prob_full, log_total = prob_table(queries, key_rows, allowed, None)
    prob_half = prob_full.astype(jnp.bfloat16)
    attended = jnp.einsum('hrk,khe->rhe', to_float(prob_half), head_split(value_rows))
    return (attended.reshape(queries.shape[0], H * HD).astype(jnp.bfloat16), log_total)

def attend_backward(queries, key_rows, value_rows, allowed, log_total, attended, grad_attn):
    row_count = queries.shape[0]
    key_count = key_rows.shape[0]
    score_scale = 1.0 / math.sqrt(HD)
    prob_full, unused_total = prob_table(queries, key_rows, allowed, log_total)
    prob_half = prob_full.astype(jnp.bfloat16)
    grad_heads = head_split(grad_attn)
    row_delta = lax.optimization_barrier(jnp.sum(grad_heads * head_split(attended), axis=-1))
    d_probs = jnp.einsum('rhe,khe->hrk', grad_heads, head_split(value_rows))
    d_scores = prob_full * (d_probs - jnp.transpose(row_delta)[..., None])
    grad_scores = to_float((d_scores * score_scale).astype(jnp.bfloat16))
    d_query = jnp.einsum('hrk,khe->rhe', grad_scores, head_split(key_rows)).reshape(row_count, H * HD)
    d_keys = jnp.einsum('hrk,rhe->khe', grad_scores, head_split(queries)).reshape(key_count, H * HD)
    d_values = jnp.einsum('hrk,rhe->khe', to_float(prob_half), grad_heads).reshape(key_count, H * HD)
    return (d_query, d_keys, d_values)

def device_partial(left_rows, right_rows):
    left_dev = to_float(left_rows).reshape(N_SHARD, TOK_DEV, left_rows.shape[1])
    right_dev = to_float(right_rows).reshape(N_SHARD, TOK_DEV, right_rows.shape[1])
    return lax.optimization_barrier(jnp.sum(round_trip(jnp.einsum('sti,stj->sij', left_dev, right_dev)), axis=0))

def device_rows(row_data):
    block_sums = lax.optimization_barrier(jnp.sum(row_data.reshape(N_SHARD, TOK_DEV, row_data.shape[1]), axis=1))
    return lax.optimization_barrier(jnp.sum(round_trip(block_sums), axis=0))

def group_pass(rows_in, cot_rows, seg_rows, halves, small_used):
    half_qkv, half_out, half_fc, half_proj = halves
    gain_one = small_used[0]
    shift_one = small_used[1]
    q_bias = small_used[2]
    v_bias = small_used[3]
    out_bias = small_used[4]
    gain_two = small_used[5]
    shift_two = small_used[6]
    fc_bias = small_used[7:11].reshape(FF)
    proj_bias = small_used[11]
    x_rows = to_float(rows_in)
    normed_one, inv_one, ln_one = norm_forward(x_rows, gain_one, shift_one)
    ln_one_half = ln_one.astype(jnp.bfloat16)
    qkv_rows = matmul(ln_one_half, half_qkv) + jnp.concatenate([q_bias, jnp.zeros((D,), jnp.float32), v_bias])
    queries = qkv_rows[:, :D].astype(jnp.bfloat16)
    key_rows = qkv_rows[:, D:2 * D].astype(jnp.bfloat16)
    value_rows = qkv_rows[:, 2 * D:].astype(jnp.bfloat16)
    position = jnp.arange(GROUP, dtype=jnp.int32)
    allowed = (seg_rows[:, None] == seg_rows[None, :]) & (position[None, :] <= position[:, None]) & ((seg_rows >= 0)[:, None] | (position[None, :] == position[:, None]))
    attended, log_total = attend_forward(queries, key_rows, value_rows, allowed)
    resid = x_rows + matmul(attended, half_out) + out_bias
    normed_two, inv_two, ln_two = norm_forward(resid, gain_two, shift_two)
    ln_two_half = ln_two.astype(jnp.bfloat16)
    pre_act = matmul(ln_two_half, half_fc) + fc_bias
    act_half = jax.nn.gelu(pre_act, approximate=False).astype(jnp.bfloat16)
    out_rows = (resid + matmul(act_half, half_proj) + proj_bias).astype(jnp.bfloat16)
    valid = (seg_rows >= 0).astype(jnp.float32)
    grad_z = to_float(cot_rows) * valid[:, None]
    gz_half = grad_z.astype(jnp.bfloat16)
    d_pre = back_product(gz_half, half_proj) * gelu_slope(pre_act)
    gu_half = d_pre.astype(jnp.bfloat16)
    d_ln_two = back_product(gu_half, half_fc)
    d_resid = grad_z + norm_backward(d_ln_two, normed_two, inv_two, gain_two)
    gh_half = d_resid.astype(jnp.bfloat16)
    grad_attn = back_product(gh_half, half_out).astype(jnp.bfloat16)
    d_query, d_keys, d_values = attend_backward(queries, key_rows, value_rows, allowed, log_total, attended, grad_attn)
    gqkv_half = jnp.concatenate([d_query, d_keys, d_values], axis=1).astype(jnp.bfloat16)
    d_ln_one = back_product(gqkv_half, half_qkv)
    grad_in = (d_resid + norm_backward(d_ln_one, normed_one, inv_one, gain_one)).astype(jnp.bfloat16)
    small_rows = jnp.stack([device_rows(d_ln_one * normed_one), device_rows(d_ln_one), device_rows(d_query), device_rows(d_values), device_rows(d_resid), device_rows(d_ln_two * normed_two), device_rows(d_ln_two)])
    small_grad = jnp.concatenate([small_rows, device_rows(d_pre).reshape(4, D), device_rows(grad_z)[None]], axis=0)
    partials = (device_partial(ln_one_half, gqkv_half), device_partial(attended, gh_half), device_partial(ln_two_half, gu_half), device_partial(act_half, gz_half), small_grad)
    return (out_rows, grad_in, partials)

def adam_update(weight, moment_one, moment_two, gradient, decay_rate):
    moment_new = BETA_ONE * moment_one + (1.0 - BETA_ONE) * gradient
    second_new = BETA_TWO * moment_two + (1.0 - BETA_TWO) * gradient * gradient
    moment_hat = moment_new / (1.0 - BETA_ONE ** STEP)
    second_hat = second_new / (1.0 - BETA_TWO ** STEP)
    weight_new = weight - LEARN_RATE * (moment_hat / (jnp.sqrt(second_hat) + ADAM_EPS) + decay_rate * weight)
    return (weight_new, moment_new, second_new)

def reference(tokens_in, cotangent, segment_ids, w_qkv, w_attn_out, w_fc, w_proj, small_w, moment_qkv, moment_attn_out, moment_fc, moment_proj, moment_small, second_qkv, second_attn_out, second_fc, second_proj, second_small):
    halves = (w_qkv.astype(jnp.bfloat16), w_attn_out.astype(jnp.bfloat16), w_fc.astype(jnp.bfloat16), w_proj.astype(jnp.bfloat16))
    small_used = round_trip(small_w)
    zero_grads = (jnp.zeros((D, 3 * D), jnp.float32), jnp.zeros((D, D), jnp.float32), jnp.zeros((D, FF), jnp.float32), jnp.zeros((FF, D), jnp.float32), jnp.zeros((12, D), jnp.float32))

    def group_step(running, inputs):
        rows_in, cot_rows, seg_rows = inputs
        out_rows, grad_in, partials = group_pass(rows_in, cot_rows, seg_rows, halves, small_used)
        return (tuple((run_sum + part_sum for run_sum, part_sum in zip(running, partials))), (out_rows, grad_in))
    totals, stacked = lax.scan(group_step, zero_grads, (tokens_in.reshape(N_DP, GROUP, D), cotangent.reshape(N_DP, GROUP, D), segment_ids.reshape(N_DP, GROUP)))
    out_act = stacked[0].reshape(TOKENS, D)
    grad_input = stacked[1].reshape(TOKENS, D)
    upd_qkv = adam_update(w_qkv, moment_qkv, second_qkv, totals[0], WEIGHT_DECAY)
    upd_out = adam_update(w_attn_out, moment_attn_out, second_attn_out, totals[1], WEIGHT_DECAY)
    upd_fc = adam_update(w_fc, moment_fc, second_fc, totals[2], WEIGHT_DECAY)
    upd_proj = adam_update(w_proj, moment_proj, second_proj, totals[3], WEIGHT_DECAY)
    upd_small = adam_update(small_w, moment_small, second_small, totals[4], 0.0)
    return (out_act, grad_input, totals[0], totals[1], totals[2], totals[3], totals[4], upd_qkv[0], upd_out[0], upd_fc[0], upd_proj[0], upd_small[0], upd_qkv[1], upd_out[1], upd_fc[1], upd_proj[1], upd_small[1], upd_qkv[2], upd_out[2], upd_fc[2], upd_proj[2], upd_small[2])
```

```python
import math

import jax
import jax.numpy as jnp
from jax import lax
from jax.experimental import pallas as pl
from jax.experimental.pallas import tpu as pltpu
from jax.sharding import PartitionSpec as P

D = 1088
H = 17
HD = 64
FF = 4352
STEP = 3


NORM_EPS = 1e-05
LEARN_RATE = 0.01
BETA_ONE = 0.9
BETA_TWO = 0.95
ADAM_EPS = 1e-08
WEIGHT_DECAY = 0.1


def outer_sum(left_rows, right_rows):
    return lax.dot_general(
        left_rows, right_rows, (((0,), (0,)), ((), ())), preferred_element_type=jnp.float32
    )


def back_product(left_rows, right_rows):
    return lax.dot_general(
        left_rows, right_rows, (((1,), (1,)), ((), ())), preferred_element_type=jnp.float32
    )


def matmul(left_rows, right_rows):
    return jnp.dot(left_rows, right_rows, preferred_element_type=jnp.float32)


def norm_forward(row_data, gain_row, shift_row):
    row_mean = jnp.mean(row_data, axis=-1, keepdims=True)
    centered = row_data - row_mean
    variance = jnp.mean(centered * centered, axis=-1, keepdims=True)
    inverse_dev = lax.rsqrt(variance + NORM_EPS)
    normed = centered * inverse_dev
    return (normed, inverse_dev, normed * gain_row + shift_row)


def norm_backward(grad_rows, normed, inverse_dev, gain_row):
    scaled = grad_rows * gain_row
    return inverse_dev * (
        scaled
        - jnp.mean(scaled, axis=-1, keepdims=True)
        - normed * jnp.mean(scaled * normed, axis=-1, keepdims=True)
    )


def gelu_slope(pre_act):
    normal_cdf = 0.5 * (1.0 + lax.erf(pre_act * 0.7071067811865476))
    normal_pdf = jnp.exp(-0.5 * pre_act * pre_act) * 0.3989422804014327
    return normal_cdf + pre_act * normal_pdf


def head_split(rows_in):
    return rows_in.reshape(rows_in.shape[0], H, HD)


def prob_table(queries, key_rows, allowed, log_total):
    score_scale = 1.0 / math.sqrt(HD)
    scores = (
        jnp.einsum(
            "rhe,khe->hrk",
            head_split(queries),
            head_split(key_rows),
            preferred_element_type=jnp.float32,
        )
        * score_scale
    )
    if log_total is None:
        exp_scores = jnp.where(allowed[None], jnp.exp(scores), 0.0)
        log_total = jnp.log(jnp.sum(exp_scores, axis=-1))
    prob_full = jnp.where(allowed[None], jnp.exp(scores - log_total[..., None]), 0.0)
    return (prob_full, log_total)


def attend_forward(queries, key_rows, value_rows, allowed):
    prob_full, log_total = prob_table(queries, key_rows, allowed, None)
    prob_half = prob_full.astype(jnp.bfloat16)
    attended = jnp.einsum(
        "hrk,khe->rhe", prob_half, head_split(value_rows), preferred_element_type=jnp.float32
    )
    return (attended.reshape(queries.shape[0], H * HD).astype(jnp.bfloat16), log_total)


def attend_backward(queries, key_rows, value_rows, allowed, log_total, attended, grad_attn):
    row_count = queries.shape[0]
    key_count = key_rows.shape[0]
    score_scale = 1.0 / math.sqrt(HD)
    prob_full, unused_total = prob_table(queries, key_rows, allowed, log_total)
    prob_half = prob_full.astype(jnp.bfloat16)
    grad_heads = head_split(grad_attn)
    row_delta = jnp.sum(
        grad_heads.astype(jnp.float32) * head_split(attended).astype(jnp.float32), axis=-1
    )
    d_probs = jnp.einsum(
        "rhe,khe->hrk", grad_heads, head_split(value_rows), preferred_element_type=jnp.float32
    )
    d_scores = prob_full * (d_probs - jnp.transpose(row_delta)[..., None])
    grad_scores = (d_scores * score_scale).astype(jnp.bfloat16)
    d_query = jnp.einsum(
        "hrk,khe->rhe", grad_scores, head_split(key_rows), preferred_element_type=jnp.float32
    ).reshape(row_count, H * HD)
    d_keys = jnp.einsum(
        "hrk,rhe->khe", grad_scores, head_split(queries), preferred_element_type=jnp.float32
    ).reshape(key_count, H * HD)
    d_values = jnp.einsum(
        "hrk,rhe->khe", prob_half, grad_heads, preferred_element_type=jnp.float32
    ).reshape(key_count, H * HD)
    return (d_query, d_keys, d_values)


def adam_update(weight, moment_one, moment_two, gradient, decay_rate):
    moment_new = BETA_ONE * moment_one + (1.0 - BETA_ONE) * gradient
    second_new = BETA_TWO * moment_two + (1.0 - BETA_TWO) * gradient * gradient
    moment_hat = moment_new / (1.0 - BETA_ONE**STEP)
    second_hat = second_new / (1.0 - BETA_TWO**STEP)
    weight_new = weight - LEARN_RATE * (
        moment_hat / (jnp.sqrt(second_hat) + ADAM_EPS) + decay_rate * weight
    )
    return (weight_new, moment_new, second_new)


LANES = 128


def pad_rows(rows_in, count):
    return jnp.pad(rows_in, ((0, count - rows_in.shape[0]), (0, 0)))


def eight(count):
    return -(-count // 8) * 8


def tiles_of(piece):
    blocks = piece.shape[1] // LANES
    return jnp.concatenate(
        [piece[:, i * LANES : (i + 1) * LANES] for i in range(blocks)], axis=0
    )


def rest_rows(count, width):
    return -(-count // (LANES // width)) if width else 0


def rest_of(rest):
    count, width = rest.shape[-2:]
    fold = LANES // width
    rows = rest_rows(count, width)
    lead = rest.shape[:-2]
    rest = jnp.pad(rest, [(0, 0)] * len(lead) + [(0, fold * rows - count), (0, 0)])
    return jnp.swapaxes(rest.reshape(lead + (fold, rows, width)), -3, -2).reshape(
        lead + (rows, LANES)
    )


def rest_back(packed, count, width):
    fold = LANES // width
    lead, rows = packed.shape[:-2], packed.shape[-2]
    rest = jnp.swapaxes(packed.reshape(lead + (rows, fold, width)), -3, -2)
    return rest.reshape(lead + (fold * rows, width))[..., :count, :]


def by_shard(rows_in, parts):
    width = rows_in.shape[1] // parts
    main = width // LANES * LANES
    cuts = [rows_in[:, i * width : i * width + main] for i in range(parts)]
    cuts += [rows_in[:, i * width + main : (i + 1) * width] for i in range(parts)]
    return jnp.concatenate(cuts, axis=1)


def by_index(rows_in, parts):
    width = rows_in.shape[1] // parts
    main = width // LANES * LANES
    rest = width - main
    cuts = []
    for i in range(parts):
        cuts.append(rows_in[:, i * main : (i + 1) * main])
        cuts.append(rows_in[:, parts * main + i * rest : parts * main + (i + 1) * rest])
    return jnp.concatenate(cuts, axis=1)


def join_kernel(plan, tiles_ref, *refs):
    rest_refs, out_refs = refs[: len(plan)], refs[len(plan) :]
    for (start, count, blocks), rest_ref, out_ref in zip(plan, rest_refs, out_refs):
        parts = tiles_ref.shape[1]
        for i in range(parts):
            for j in range(blocks):
                lane = (i * blocks + j) * LANES
                out_ref[0, :, lane : lane + LANES] = tiles_ref[
                    0, i, start + j * count : start + (j + 1) * count, :
                ]
        out_ref[0, :, parts * blocks * LANES :] = rest_ref[0]


def join_tiles(gathered, plan, rests):
    n_dp, parts, rows, lanes = gathered.shape
    shapes = [
        (n_dp, count, parts * blocks * LANES + rest.shape[-1])
        for (start, count, blocks), rest in zip(plan, rests)
    ]
    return pl.pallas_call(
        lambda *refs: join_kernel(plan, *refs),
        grid=(n_dp,),
        in_specs=[pl.BlockSpec((1, parts, rows, lanes), lambda d: (d, 0, 0, 0))]
        + [pl.BlockSpec((1,) + rest.shape[1:], lambda d: (d, 0, 0)) for rest in rests],
        out_specs=[pl.BlockSpec((1,) + shape[1:], lambda d: (d, 0, 0)) for shape in shapes],
        out_shape=[jax.ShapeDtypeStruct(shape, gathered.dtype) for shape in shapes],
        compiler_params=pltpu.CompilerParams(vmem_limit_bytes=40 * 1024 * 1024),
    )(gathered, *rests)


def cut_kernel(plan, rest_starts, *refs):
    pairs = len(plan)
    left_refs, right_refs = refs[:pairs], refs[pairs : 2 * pairs]
    rest_refs, out_ref = refs[2 * pairs : -1], refs[-1]
    parts = out_ref.shape[1]
    for (start, count, blocks), left_ref, right_ref in zip(plan, left_refs, right_refs):
        for i in range(parts):
            width = blocks * LANES
            product = jnp.dot(
                left_ref[0],
                right_ref[:, i * width : (i + 1) * width],
                preferred_element_type=jnp.float32,
            ).astype(out_ref.dtype)
            for j in range(blocks):
                out_ref[0, i, start + j * count : start + (j + 1) * count, :] = product[
                    :, j * LANES : (j + 1) * LANES
                ]
    for start, rest_ref in zip(rest_starts, rest_refs):
        for i in range(parts):
            out_ref[0, i, start : start + rest_ref.shape[2], :] = rest_ref[0, i]


def cut_tiles(left_list, right_list, plan, rest_list, rest_starts, rows):
    n_dp, parts = rest_list[0].shape[:2]
    lefts = [
        left.T.reshape(n_dp, count, left.shape[0])
        for left, (start, count, blocks) in zip(left_list, plan)
    ]
    return pl.pallas_call(
        lambda *refs: cut_kernel(plan, rest_starts, *refs),
        grid=(n_dp,),
        in_specs=[pl.BlockSpec((1,) + left.shape[1:], lambda d: (d, 0, 0)) for left in lefts]
        + [pl.BlockSpec(right.shape, lambda d: (0, 0)) for right in right_list]
        + [pl.BlockSpec((1,) + rest.shape[1:], lambda d: (d, 0, 0, 0)) for rest in rest_list],
        out_specs=pl.BlockSpec((1, parts, rows, LANES), lambda d: (d, 0, 0, 0)),
        out_shape=jax.ShapeDtypeStruct((n_dp, parts, rows, LANES), jnp.bfloat16),
        compiler_params=pltpu.CompilerParams(vmem_limit_bytes=40 * 1024 * 1024),
    )(*lefts, *right_list, *rest_list)


def on_device_general(
    tokens_in,
    cotangent,
    segment_ids,
    w_qkv,
    w_attn_out,
    w_fc,
    w_proj,
    small_w,
    moment_qkv,
    moment_attn_out,
    moment_fc,
    moment_proj,
    moment_small,
    second_qkv,
    second_attn_out,
    second_fc,
    second_proj,
    second_small,
):
    axes = ("dp", "shard")
    n_dp = lax.axis_size("dp")
    n_shard = lax.axis_size("shard")
    rows_own, cols_qkv = w_qkv.shape
    cols_out = w_attn_out.shape[1]
    cols_fc = w_fc.shape[1]
    cols_proj = w_proj.shape[1]
    rows_proj = w_proj.shape[0]
    main_own = rows_own // LANES * LANES
    main_proj = rows_proj // LANES * LANES
    rest_own, rest_proj = rows_own - main_own, rows_proj - main_proj
    col_list = (cols_qkv, cols_out, cols_fc)
    col_sum = sum(col_list)
    sizes = [count * (main_own // LANES) for count in col_list]
    sizes += [cols_proj * (main_proj // LANES)]
    sizes += [eight(rest_rows(col_sum, rest_own)), eight(rest_rows(cols_proj, rest_proj))]
    starts = [sum(sizes[:i]) for i in range(len(sizes) + 1)]
    pieces = [w.astype(jnp.bfloat16).T for w in (w_qkv, w_attn_out, w_fc)]
    piece_proj = w_proj.astype(jnp.bfloat16).T
    rest_one = jnp.concatenate([piece[:, main_own:] for piece in pieces], axis=0)
    small_count = small_w.shape[0] * rows_own
    small_tiles = eight(-(-small_count // LANES))
    small_flat = jnp.pad(
        small_w.astype(jnp.bfloat16).reshape(small_count), (0, small_tiles * LANES - small_count)
    )
    packed = jnp.concatenate(
        [tiles_of(piece[:, :main_own]) for piece in pieces]
        + [
            tiles_of(piece_proj[:, :main_proj]),
            pad_rows(rest_of(rest_one), sizes[4]),
            pad_rows(rest_of(piece_proj[:, main_proj:]), sizes[5]),
            small_flat.reshape(small_tiles, LANES),
        ],
        axis=0,
    )
    gathered = lax.all_gather(packed, axes, axis=0, tiled=False).reshape(
        n_dp, n_shard, packed.shape[0], LANES
    )

    def rows_at(start, count):
        return lax.slice_in_dim(gathered, start, start + count, axis=2)

    all_rest = jnp.swapaxes(
        rest_back(rows_at(starts[4], rest_rows(col_sum, rest_own)), col_sum, rest_own), 1, 2
    ).reshape(n_dp, col_sum, n_shard * rest_own)

    proj_rest = jnp.swapaxes(
        rest_back(rows_at(starts[5], rest_rows(cols_proj, rest_proj)), cols_proj, rest_proj), 1, 2
    ).reshape(n_dp, cols_proj, n_shard * rest_proj)
    own_blocks = main_own // LANES
    plan = [
        (starts[0], cols_qkv, own_blocks),
        (starts[1], cols_out, own_blocks),
        (starts[2], cols_fc, own_blocks),
        (starts[3], cols_proj, main_proj // LANES),
    ]
    rests = [
        all_rest[:, :cols_qkv],
        all_rest[:, cols_qkv : cols_qkv + cols_out],
        all_rest[:, cols_qkv + cols_out :],
        proj_rest,
    ]
    full_qkv, full_out, full_fc, full_proj = (
        full.reshape(full.shape[0] * full.shape[1], full.shape[2])
        for full in join_tiles(gathered, plan, rests)
    )
    full_small = jnp.transpose(
        gathered[0, :, starts[6] :]
        .reshape(n_shard, small_tiles * LANES)[:, :small_count]
        .reshape(n_shard, small_w.shape[0], rows_own),
        (1, 0, 2),
    ).reshape(small_w.shape[0], n_shard * rows_own)
    small_vals = full_small.astype(jnp.float32)
    gain_one = small_vals[0]
    shift_one = small_vals[1]
    q_bias = small_vals[2]
    v_bias = small_vals[3]
    out_bias = small_vals[4]
    gain_two = small_vals[5]
    shift_two = small_vals[6]
    fc_bias = small_vals[7:11].reshape(FF)
    proj_bias = small_vals[11]
    tok_rows = tokens_in.shape[0]
    group_size = segment_ids.shape[0]
    shard_index = lax.axis_index("shard")
    own_seg = lax.dynamic_slice_in_dim(segment_ids, shard_index * tok_rows, tok_rows)
    query_pos = shard_index * tok_rows + jnp.arange(tok_rows, dtype=jnp.int32)
    x_rows = tokens_in.astype(jnp.float32)
    normed_one, inv_one, ln_one = norm_forward(x_rows, gain_one, shift_one)
    ln_one_half = ln_one.astype(jnp.bfloat16)
    ln_one_cut = by_shard(ln_one_half, n_shard)
    qkv_rows = back_product(ln_one_cut, full_qkv) + jnp.concatenate(
        [q_bias, jnp.zeros_like(q_bias), v_bias]
    )
    queries = qkv_rows[:, :D].astype(jnp.bfloat16)
    kv_half = qkv_rows[:, D:].astype(jnp.bfloat16)
    kv_all = lax.all_gather(kv_half, "shard", axis=0, tiled=True)
    key_all = kv_all[:, :D]
    value_all = kv_all[:, D:]
    key_pos = jnp.arange(group_size, dtype=jnp.int32)
    allowed = (
        (own_seg[:, None] == segment_ids[None, :])
        & (key_pos[None, :] <= query_pos[:, None])
        & ((own_seg >= 0)[:, None] | (key_pos[None, :] == query_pos[:, None]))
    )
    attended, log_total = attend_forward(queries, key_all, value_all, allowed)
    attended_cut = by_shard(attended, n_shard)
    resid = x_rows + back_product(attended_cut, full_out) + out_bias
    normed_two, inv_two, ln_two = norm_forward(resid, gain_two, shift_two)
    ln_two_half = ln_two.astype(jnp.bfloat16)
    ln_two_cut = by_shard(ln_two_half, n_shard)
    pre_act = back_product(ln_two_cut, full_fc) + fc_bias
    act_half = jax.nn.gelu(pre_act, approximate=False).astype(jnp.bfloat16)
    act_cut = by_shard(act_half, n_shard)
    out_act = (resid + back_product(act_cut, full_proj) + proj_bias).astype(jnp.bfloat16)
    valid = (own_seg >= 0).astype(jnp.float32)
    grad_z = cotangent.astype(jnp.float32) * valid[:, None]
    gz_half = grad_z.astype(jnp.bfloat16)
    d_pre = by_index(matmul(gz_half, full_proj), n_shard) * gelu_slope(pre_act)
    gu_half = d_pre.astype(jnp.bfloat16)
    d_ln_two = by_index(matmul(gu_half, full_fc), n_shard)
    d_resid = grad_z + norm_backward(d_ln_two, normed_two, inv_two, gain_two)
    gh_half = d_resid.astype(jnp.bfloat16)
    grad_attn = by_index(matmul(gh_half, full_out).astype(jnp.bfloat16), n_shard)
    d_query, d_keys_all, d_values_all = attend_backward(
        queries, key_all, value_all, allowed, log_total, attended, grad_attn
    )
    d_kv = lax.psum_scatter(
        jnp.concatenate(
            [d_keys_all.astype(jnp.bfloat16), d_values_all.astype(jnp.bfloat16)], axis=1
        ),
        "shard",
        scatter_dimension=0,
        tiled=True,
    )
    d_values = d_kv[:, D:].astype(jnp.float32)
    gqkv_half = jnp.concatenate([d_query.astype(jnp.bfloat16), d_kv], axis=1)
    d_ln_one = by_index(matmul(gqkv_half, full_qkv), n_shard)
    grad_input = (d_resid + norm_backward(d_ln_one, normed_one, inv_one, gain_one)).astype(
        jnp.bfloat16
    )
    small_rows = jnp.stack(
        [
            jnp.sum(d_ln_one * normed_one, axis=0),
            jnp.sum(d_ln_one, axis=0),
            jnp.sum(d_query, axis=0),
            jnp.sum(d_values, axis=0),
            jnp.sum(d_resid, axis=0),
            jnp.sum(d_ln_two * normed_two, axis=0),
            jnp.sum(d_ln_two, axis=0),
        ]
    )
    small_grad = jnp.concatenate(
        [small_rows, jnp.sum(d_pre, axis=0).reshape(4, D), jnp.sum(grad_z, axis=0)[None]], axis=0
    )
    lefts = (gqkv_half, gh_half, gu_half, gz_half)
    rights = (ln_one_cut, attended_cut, ln_two_cut, act_cut)

    def rest_cut(left, right, main, rest):
        product = outer_sum(left, right[:, n_shard * main :]).astype(jnp.bfloat16)
        count = product.shape[0] // n_dp
        return jnp.swapaxes(product.reshape(n_dp, count, n_shard, rest), 1, 2)

    def fill(packed_rest, count):
        return jnp.pad(
            packed_rest, ((0, 0), (0, 0), (0, count - packed_rest.shape[2]), (0, 0))
        )

    outgoing = cut_tiles(
        lefts,
        rights,
        plan,
        [
            fill(
                rest_of(
                    jnp.concatenate(
                        [
                            rest_cut(left, right, main_own, rest_own)
                            for left, right in zip(lefts[:3], rights[:3])
                        ],
                        axis=2,
                    )
                ),
                sizes[4],
            ),
            fill(rest_of(rest_cut(gz_half, act_cut, main_proj, rest_proj)), sizes[5]),
        ],
        starts[4:6],
        starts[6],
    ).reshape(n_dp * n_shard, starts[6], LANES)
    summed = lax.psum_scatter(outgoing, axes, scatter_dimension=0, tiled=False).astype(
        jnp.float32
    )

    def owned(start, count, main, rest):
        blocks = main // LANES
        cuts = [summed[start + i * count : start + (i + 1) * count] for i in range(blocks)]
        return jnp.concatenate(cuts + [rest], axis=1).T

    sum_rest = rest_back(
        summed[starts[4] : starts[4] + rest_rows(col_sum, rest_own)], col_sum, rest_own
    )
    grad_qkv = owned(starts[0], cols_qkv, main_own, sum_rest[:cols_qkv])
    grad_attn_out = owned(
        starts[1], cols_out, main_own, sum_rest[cols_qkv : cols_qkv + cols_out]
    )
    grad_fc = owned(starts[2], cols_fc, main_own, sum_rest[cols_qkv + cols_out :])
    grad_proj = owned(
        starts[3],
        cols_proj,
        main_proj,
        rest_back(
            summed[starts[5] : starts[5] + rest_rows(cols_proj, rest_proj)], cols_proj, rest_proj
        ),
    )
    small_total = lax.psum(small_grad.astype(jnp.bfloat16).astype(jnp.float32), axes)
    grad_small = lax.dynamic_slice_in_dim(
        small_total, shard_index * rows_own, rows_own, axis=1
    )
    upd_qkv = adam_update(w_qkv, moment_qkv, second_qkv, grad_qkv, WEIGHT_DECAY)
    upd_out = adam_update(w_attn_out, moment_attn_out, second_attn_out, grad_attn_out, WEIGHT_DECAY)
    upd_fc = adam_update(w_fc, moment_fc, second_fc, grad_fc, WEIGHT_DECAY)
    upd_proj = adam_update(w_proj, moment_proj, second_proj, grad_proj, WEIGHT_DECAY)
    upd_small = adam_update(small_w, moment_small, second_small, grad_small, 0.0)
    return (
        out_act,
        grad_input,
        grad_qkv,
        grad_attn_out,
        grad_fc,
        grad_proj,
        grad_small,
        upd_qkv[0],
        upd_out[0],
        upd_fc[0],
        upd_proj[0],
        upd_small[0],
        upd_qkv[1],
        upd_out[1],
        upd_fc[1],
        upd_proj[1],
        upd_small[1],
        upd_qkv[2],
        upd_out[2],
        upd_fc[2],
        upd_proj[2],
        upd_small[2],
    )


AXES = ("dp", "shard")
MESH_ID = pl.DeviceIdType.MESH
COLS = 2
PIECES = 3


def place():
    d = lax.axis_index("dp")
    s = lax.axis_index("shard")
    z, y = d // COLS, d % COLS
    x, c = s // 2, s % 2
    x_dev = (d, (1 - x) * 2 + c)
    y_dev = (z * COLS + 1 - y, s)
    near = tuple(a * (1 - c) + b * c for a, b in zip(x_dev, y_dev))
    far = tuple(b * (1 - c) + a * c for a, b in zip(x_dev, y_dev))
    up = (d + COLS, s)
    down = (d - COLS, s)
    sib = (d, x * 2 + 1 - c)
    return d, s, z, y, x, c, near, far, up, down, sib


def flip(value, change):
    return value + change - 2 * value * change


def enter(n_dp, n_shard, d, s):
    barrier = pltpu.get_barrier_semaphore()
    for step in range(1, n_dp):
        pl.semaphore_signal(
            barrier, inc=1, device_id=((d + step) % n_dp, s), device_id_type=MESH_ID
        )
    for step in range(1, n_shard):
        pl.semaphore_signal(
            barrier, inc=1, device_id=(d, (s + step) % n_shard), device_id_type=MESH_ID
        )
    pl.semaphore_wait(barrier, n_dp + n_shard - 2)


def gather_kernel(
    n_dp,
    n_shard,
    cut_ref,
    proj_ref,
    small_ref,
    full_ref,
    small_out,
    own,
    swap,
    local_sem,
    swap_sem,
    small_sem,
    send_sem,
    recv_sem,
    sib_sem,
):
    d, s, z, y, x, c, near, far, up, down, sib = place()
    depth = n_dp // COLS
    lanes = cut_ref.shape[-1]

    def where(zs, fa, fb):
        fx = fa * (1 - c) + fb * c
        fy = fb * (1 - c) + fa * c
        return zs * COLS + flip(y, fy), flip(x, fx) * 2 + c

    def number(zs, fa, fb, k):
        return ((zs * 2 + fa) * 2 + fb) * PIECES + k

    def copy(kind, zs, fa, fb, k, src=None):
        dp, sh = where(zs, fa, fb)
        block = full_ref.at[dp, sh, k]
        target = (near, far, up, down, sib)[kind]
        mine = number(zs, fa, fb, k)
        if kind == 4:
            arrive = sib_sem.at[mine]
        else:
            arrive = recv_sem.at[number(zs, 1 if kind == 0 else fa, 1 if kind == 1 else fb, k)]
        return pltpu.make_async_remote_copy(
            src_ref=block if src is None else src,
            dst_ref=block,
            send_sem=send_sem.at[kind, mine],
            recv_sem=arrive,
            device_id=target,
            device_id_type=MESH_ID,
        )

    def arrived(zs, fa, fb, k):
        dp, sh = where(zs, fa, fb)
        block = full_ref.at[dp, sh, k]
        pltpu.make_async_copy(block, block, recv_sem.at[number(zs, fa, fb, k)]).wait()

    enter(n_dp, n_shard, d, s)

    def swap_copy(step):
        peer = (s + step) % n_shard
        return pltpu.make_async_remote_copy(
            src_ref=cut_ref.at[peer],
            dst_ref=swap.at[s],
            send_sem=swap_sem.at[0, step],
            recv_sem=swap_sem.at[1, step],
            device_id=(d, peer),
            device_id_type=MESH_ID,
        )

    def small_copy(step):
        peer = (s + step) % n_shard
        return pltpu.make_async_remote_copy(
            src_ref=small_ref,
            dst_ref=small_out.at[s],
            send_sem=small_sem.at[0, step],
            recv_sem=small_sem.at[1, step],
            device_id=(d, peer),
            device_id_type=MESH_ID,
        )

    for step in range(1, n_shard):
        swap_copy(step).start()
    own_cut = pltpu.make_async_copy(cut_ref.at[s], swap.at[s], local_sem.at[0])
    own_cut.start()
    own_small = pltpu.make_async_copy(small_ref, small_out.at[s], local_sem.at[1])
    own_small.start()

    def spread(k, src):
        copy(0, z, 0, 0, k, src).start()
        copy(1, z, 0, 0, k, src).start()

        @pl.when(z < depth - 1)
        def _():
            copy(2, z, 0, 0, k, src).start()

        @pl.when(z > 0)
        def _():
            copy(3, z, 0, 0, k, src).start()

        copy(4, z, 0, 0, k, src).start()
        keep = pltpu.make_async_copy(src, full_ref.at[d, s, k], local_sem.at[2 + k])
        keep.start()

    spread(2, proj_ref)
    for step in range(1, n_shard):
        small_copy(step).start()
    own_cut.wait()
    for step in range(1, n_shard):
        swap_copy(step).wait()
    for k in (1, 0):
        for part in range(n_shard):
            own[k, :, part * lanes : (part + 1) * lanes] = swap[part, k]
    spread(1, own.at[1])
    spread(0, own.at[0])

    def pass_on(zs, fa, k, go_up, go_down, go_near):
        arrived(zs, fa, 0, k)
        if go_up:

            @pl.when(z < depth - 1)
            def _():
                copy(2, zs, fa, 0, k).start()

        if go_down:

            @pl.when(z > 0)
            def _():
                copy(3, zs, fa, 0, k).start()

        if go_near:
            copy(0, zs, fa, 0, k).start()
        copy(1, zs, fa, 0, k).start()
        copy(4, zs, fa, 0, k).start()

    def from_near(zs):
        pass_on(zs, 1, 0, False, False, False)

    def from_far(zs):
        def step(j, carry):
            fa, k = j // PIECES, PIECES - 1 - j % PIECES
            arrived(zs, fa, 1, k)
            copy(4, zs, fa, 1, k).start()
            return carry

        lax.fori_loop(0, 2 * PIECES, step, 0)

    pass_on(z, 1, 2, True, True, False)
    pass_on(z, 1, 1, True, True, False)
    from_near(z)
    for delta in range(1, depth):
        for sign in (-1, 1):
            zs = z + sign * delta

            @pl.when((zs >= 0) & (zs < depth))
            def _():
                for k, fa in ((2, 0), (1, 0), (0, 0), (2, 1), (1, 1)):
                    pass_on(zs, fa, k, sign < 0, sign > 0, k == 0)

        for sign in (-1, 1):
            zs = z + sign * delta

            @pl.when((zs >= 0) & (zs < depth))
            def _():
                from_near(zs)

        for sign in (-1, 1) if delta > 1 else (0,):
            zs = z + sign * (delta - 1)

            @pl.when((zs >= 0) & (zs < depth))
            def _():
                from_far(zs)

    for sign in (-1, 1):
        zs = z + sign * (depth - 1)

        @pl.when((zs >= 0) & (zs < depth))
        def _():
            from_far(zs)

    own_small.wait()
    for k in range(PIECES):
        pltpu.make_async_copy(own.at[0], full_ref.at[d, s, k], local_sem.at[2 + k]).wait()
    for step in range(1, n_shard):
        small_copy(step).wait()

    def finish(zs, carry):
        for fa in range(2):
            for k in range(PIECES):
                if k > 0 or fa == 0:

                    @pl.when((z < depth - 1) & (zs <= z))
                    def _():
                        copy(2, zs, fa, 0, k).wait_send()

                    @pl.when((z > 0) & (zs >= z))
                    def _():
                        copy(3, zs, fa, 0, k).wait_send()

                if fa == 0:
                    if k == 0:
                        copy(0, zs, fa, 0, k).wait_send()
                    else:

                        @pl.when(zs == z)
                        def _():
                            copy(0, zs, fa, 0, k).wait_send()

                copy(1, zs, fa, 0, k).wait_send()
                for fb in range(2):
                    copy(4, zs, fa, fb, k).wait()
        return carry

    lax.fori_loop(0, depth, finish, 0)


def gather_rows(cut, proj, small, n_dp, n_shard):
    piece_rows, width = proj.shape
    count = n_dp // COLS * 4 * PIECES
    shape = (n_dp, n_shard, PIECES, piece_rows, width)
    return pl.pallas_call(
        lambda *refs: gather_kernel(n_dp, n_shard, *refs),
        out_shape=[
            jax.ShapeDtypeStruct(shape, cut.dtype),
            jax.ShapeDtypeStruct((n_shard,) + small.shape, small.dtype),
        ],
        in_specs=[pl.BlockSpec(memory_space=pltpu.VMEM)] * 3,
        out_specs=[
            pl.BlockSpec(memory_space=pltpu.HBM),
            pl.BlockSpec(memory_space=pltpu.VMEM),
        ],
        scratch_shapes=[
            pltpu.VMEM((PIECES - 1, piece_rows, width), cut.dtype),
            pltpu.VMEM(cut.shape, cut.dtype),
            pltpu.SemaphoreType.DMA((2 + PIECES,)),
            pltpu.SemaphoreType.DMA((2, n_shard)),
            pltpu.SemaphoreType.DMA((2, n_shard)),
            pltpu.SemaphoreType.DMA((5, count)),
            pltpu.SemaphoreType.DMA((count,)),
            pltpu.SemaphoreType.DMA((count,)),
        ],
        compiler_params=pltpu.CompilerParams(
            collective_id=0, has_side_effects=True, vmem_limit_bytes=24 * 1024 * 1024
        ),
    )(cut, proj, small)


def reduce_kernel(
    n_dp,
    n_shard,
    grad_ref,
    small_ref,
    swap_out,
    proj_out,
    small_out,
    total,
    from_sib,
    from_far,
    from_near,
    from_line,
    cut,
    small_part,
    small_sum,
    small_all,
    local_sem,
    sib_sem,
    far_sem,
    near_sem,
    line_sem,
    swap_sem,
    small_sem,
    small_dp_sem,
    own_sem,
):
    d, s, z, y, x, c, near, far, up, down, sib = place()
    depth = n_dp // COLS
    lanes = swap_out.shape[-1]
    per_level = 2 * PIECES

    def where(zq, fa, fb, core):
        fx = fa * (1 - core) + fb * core
        fy = fb * (1 - core) + fa * core
        return zq * COLS + flip(y, fy), flip(x, fx) * 2 + core

    def spot(zq, fa, fb, k):
        return ((zq * 2 + fb) * 2 + fa) * PIECES + k

    def order(j):
        level = j // per_level
        zq = (level % 2) * (depth - 1 - level // 2) + (1 - level % 2) * (level // 2)
        k = j % per_level // 2
        fa = 1 - j % 2
        return zq, fa, k

    def remote(src, dst, sems, number, target):
        return pltpu.make_async_remote_copy(
            src_ref=src,
            dst_ref=dst,
            send_sem=sems.at[0, number],
            recv_sem=sems.at[1, number],
            device_id=target,
            device_id_type=MESH_ID,
        )

    def sib_copy(zq, fa, fb, k):
        dp, sh = where(zq, fa, fb, 1 - c)
        slot = spot(zq, fa, fb, k)
        return remote(grad_ref.at[dp, sh, k], from_sib.at[slot], sib_sem, slot, sib)

    def own_copy(zq, fa, fb, k):
        dp, sh = where(zq, fa, fb, c)
        slot = spot(zq, fa, fb, k)
        return pltpu.make_async_copy(grad_ref.at[dp, sh, k], total.at[slot], local_sem.at[slot])

    def far_copy(zq, fa, k):
        slot = (zq * 2 + fa) * PIECES + k
        return remote(total.at[spot(zq, fa, 1, k)], from_far.at[slot], far_sem, slot, far)

    def near_copy(zq, k, slot):
        return remote(total.at[spot(zq, 1, 0, k)], from_near.at[slot], near_sem, slot, near)

    def line_copy(way, zq, fa, k):
        slot = (way * depth + zq) * 5 + (0 if k == 0 else 2 * k - 1 + fa)
        return remote(
            total.at[spot(zq, fa, 0, k)],
            from_line.at[slot],
            line_sem,
            slot,
            (up, down)[way],
        )

    def add(slot, other):
        total[slot] = (
            total[slot].astype(jnp.float32) + other[...].astype(jnp.float32)
        ).astype(total.dtype)

    enter(n_dp, n_shard, d, s)

    def small_shard(step):
        peer = (s + step) % n_shard
        return remote(small_ref.at[peer], small_part.at[s], small_sem, step, (d, peer))

    for step in range(1, n_shard):
        small_shard(step).start()
    own_small = pltpu.make_async_copy(small_ref.at[s], small_part.at[s], own_sem.at[0])
    own_small.start()

    def begin(fb):
        def step(j, carry):
            zq, fa, k = order(j)
            sib_copy(zq, fa, fb, k).start()
            own_copy(zq, fa, fb, k).start()
            return carry

        return step

    lax.fori_loop(0, depth * per_level, begin(1), 0)
    lax.fori_loop(0, depth * per_level, begin(0), 0)

    def merge(fb):
        def step(j, carry):
            zq, fa, k = order(j)
            own_copy(zq, fa, fb, k).wait()
            sib_copy(zq, fa, fb, k).wait_recv()
            slot = spot(zq, fa, fb, k)
            add(slot, from_sib.at[slot])
            if fb == 1:
                far_copy(zq, fa, k).start()
            return carry

        return step

    lax.fori_loop(0, depth * per_level, merge(1), 0)

    own_small.wait()
    for step in range(1, n_shard):
        small_shard(step).wait()
    small_sum[...] = jnp.sum(small_part[...], axis=0)

    def small_dp(step):
        peer = (d + step) % n_dp
        return remote(small_sum, small_all.at[d], small_dp_sem, step, (peer, s))

    lax.fori_loop(0, depth * per_level, merge(0), 0)
    for step in range(1, n_dp):
        small_dp(step).start()
    own_all = pltpu.make_async_copy(small_sum, small_all.at[d], own_sem.at[1])
    own_all.start()

    def level_step(level, carry):
        zq = (level % 2) * (depth - 1 - level // 2) + (1 - level % 2) * (level // 2)

        def line_step(fa, k):
            @pl.when(zq < z)
            def _():
                @pl.when(z < depth - 1)
                def _():
                    line_copy(1, zq, fa, k).wait_recv()
                    add(spot(zq, fa, 0, k), from_line.at[(depth + zq) * 5 + slot_of(fa, k)])

                line_copy(1, zq, fa, k).start()

            @pl.when(zq > z)
            def _():
                @pl.when(z > 0)
                def _():
                    line_copy(0, zq, fa, k).wait_recv()
                    add(spot(zq, fa, 0, k), from_line.at[zq * 5 + slot_of(fa, k)])

                line_copy(0, zq, fa, k).start()

        def slot_of(fa, k):
            return 0 if k == 0 else 2 * k - 1 + fa

        def take_far(fa, k):
            far_copy(zq, fa, k).wait_recv()
            add(spot(zq, fa, 0, k), from_far.at[(zq * 2 + fa) * PIECES + k])

        take_far(1, 0)
        near_copy(zq, 0, zq).start()
        take_far(0, 0)
        for k in (1, 2):
            for fa in (1, 0):
                take_far(fa, k)
                line_step(fa, k)
        near_copy(zq, 0, zq).wait_recv()
        add(spot(zq, 0, 0, 0), from_near.at[zq])
        line_step(0, 0)
        return carry

    lax.fori_loop(0, depth, level_step, 0)

    def last(fa, k):
        number = 0 if k == 0 else 2 * k - 1 + fa

        @pl.when(z < depth - 1)
        def _():
            line_copy(1, z, fa, k).wait_recv()
            add(spot(z, fa, 0, k), from_line.at[(depth + z) * 5 + number])

        @pl.when(z > 0)
        def _():
            line_copy(0, z, fa, k).wait_recv()
            add(spot(z, fa, 0, k), from_line.at[z * 5 + number])

    for k in (1, 2):
        last(1, k)
        near_copy(z, k, depth + k - 1).start()
    for k in (1, 0, 2):
        last(0, k)
        if k > 0:
            near_copy(z, k, depth + k - 1).wait_recv()
            add(spot(z, 0, 0, k), from_near.at[depth + k - 1])
        if k < 2:
            for part in range(n_shard):
                cut[part, k] = total[spot(z, 0, 0, k), :, part * lanes : (part + 1) * lanes]

    def swap_copy(step):
        peer = (s + step) % n_shard
        return remote(cut.at[peer], swap_out.at[s], swap_sem, step, (d, peer))

    for step in range(1, n_shard):
        swap_copy(step).start()
    own_cut = pltpu.make_async_copy(cut.at[s], swap_out.at[s], own_sem.at[2])
    own_cut.start()
    proj_out[...] = total[spot(z, 0, 0, 2)]
    own_all.wait()
    for step in range(1, n_dp):
        small_dp(step).wait()
    small_out[...] = jnp.sum(small_all[...], axis=0)
    own_cut.wait()
    for step in range(1, n_shard):
        swap_copy(step).wait()

    def finish(zq, carry):
        for k in range(PIECES):
            for fa in range(2):
                for fb in range(2):
                    sib_copy(zq, fa, fb, k).wait_send()
                far_copy(zq, fa, k).wait_send()
                if k > 0 or fa == 0:

                    @pl.when(zq < z)
                    def _():
                        line_copy(1, zq, fa, k).wait_send()

                    @pl.when(zq > z)
                    def _():
                        line_copy(0, zq, fa, k).wait_send()

        near_copy(zq, 0, zq).wait_send()
        return carry

    lax.fori_loop(0, depth, finish, 0)
    for k in (1, 2):
        near_copy(z, k, depth + k - 1).wait_send()


def reduce_rows(grads, small, n_dp, n_shard):
    piece_rows, width = grads.shape[-2:]
    lanes = width // n_shard
    depth = n_dp // COLS
    count = depth * 4 * PIECES
    kind = grads.dtype

    def pieces(number):
        return pltpu.VMEM((number, piece_rows, width), kind)

    def sems(*shape):
        return pltpu.SemaphoreType.DMA(shape)

    return pl.pallas_call(
        lambda *refs: reduce_kernel(n_dp, n_shard, *refs),
        out_shape=[
            jax.ShapeDtypeStruct((n_shard, PIECES - 1, piece_rows, lanes), kind),
            jax.ShapeDtypeStruct((piece_rows, width), kind),
            jax.ShapeDtypeStruct(small.shape[1:], small.dtype),
        ],
        in_specs=[
            pl.BlockSpec(memory_space=pltpu.HBM),
            pl.BlockSpec(memory_space=pltpu.VMEM),
        ],
        out_specs=[pl.BlockSpec(memory_space=pltpu.VMEM)] * 3,
        scratch_shapes=[
            pieces(count),
            pieces(count),
            pieces(depth * 2 * PIECES),
            pieces(depth + 2),
            pieces(2 * depth * 5),
            pltpu.VMEM((n_shard, PIECES - 1, piece_rows, lanes), kind),
            pltpu.VMEM(small.shape, small.dtype),
            pltpu.VMEM(small.shape[1:], small.dtype),
            pltpu.VMEM((n_dp,) + small.shape[1:], small.dtype),
            sems(count),
            sems(2, count),
            sems(2, depth * 2 * PIECES),
            sems(2, depth + 2),
            sems(2, 2 * depth * 5),
            sems(2, n_shard),
            sems(2, n_shard),
            sems(2, n_dp),
            sems(3),
        ],
        compiler_params=pltpu.CompilerParams(
            collective_id=1, has_side_effects=True, vmem_limit_bytes=62 * 1024 * 1024
        ),
    )(grads, small)


def fits(w_qkv, w_attn_out, w_fc, w_proj, n_dp, n_shard):
    unit = w_proj.shape[1]
    return (
        n_shard == 4
        and n_dp % COLS == 0
        and n_dp > COLS
        and unit % 8 == 0
        and w_qkv.shape[1] == 3 * unit
        and w_attn_out.shape[1] == unit
        and w_fc.shape[1] == 4 * unit
        and w_proj.shape[0] == w_qkv.shape[0] * n_shard
    )


def on_device(
    tokens_in,
    cotangent,
    segment_ids,
    w_qkv,
    w_attn_out,
    w_fc,
    w_proj,
    small_w,
    moment_qkv,
    moment_attn_out,
    moment_fc,
    moment_proj,
    moment_small,
    second_qkv,
    second_attn_out,
    second_fc,
    second_proj,
    second_small,
):
    n_dp = lax.axis_size("dp")
    n_shard = lax.axis_size("shard")
    if not fits(w_qkv, w_attn_out, w_fc, w_proj, n_dp, n_shard):
        return on_device_general(
            tokens_in,
            cotangent,
            segment_ids,
            w_qkv,
            w_attn_out,
            w_fc,
            w_proj,
            small_w,
            moment_qkv,
            moment_attn_out,
            moment_fc,
            moment_proj,
            moment_small,
            second_qkv,
            second_attn_out,
            second_fc,
            second_proj,
            second_small,
        )
    rows_own = w_qkv.shape[0]
    cols_qkv, cols_out = w_qkv.shape[1], w_attn_out.shape[1]
    unit = w_proj.shape[1]
    small_count = small_w.shape[0]
    cut = jnp.concatenate(
        [w.astype(jnp.bfloat16).T for w in (w_qkv, w_attn_out, w_fc)], axis=0
    ).reshape(n_shard, PIECES - 1, unit, rows_own)
    gathered, small_all = gather_rows(
        cut,
        w_proj.astype(jnp.bfloat16).T,
        pad_rows(small_w.astype(jnp.bfloat16), eight(small_count)),
        n_dp,
        n_shard,
    )
    units = gathered[:, :, : PIECES - 1].reshape(n_dp, n_shard * 2, unit, D)
    full_qkv = units[:, :3].reshape(3 * D, D)
    full_out = units[:, 3].reshape(D, D)
    full_fc = units[:, 4:].reshape(FF, D)
    full_proj = [gathered[:, t, PIECES - 1].reshape(D, D) for t in range(n_shard)]
    small_vals = jnp.swapaxes(small_all, 0, 1).reshape(-1, D)[:small_count].astype(jnp.float32)
    gain_one = small_vals[0]
    shift_one = small_vals[1]
    q_bias = small_vals[2]
    v_bias = small_vals[3]
    out_bias = small_vals[4]
    gain_two = small_vals[5]
    shift_two = small_vals[6]
    fc_bias = small_vals[7:11].reshape(FF)
    proj_bias = small_vals[11]
    tok_rows = tokens_in.shape[0]
    group_size = segment_ids.shape[0]
    shard_index = lax.axis_index("shard")
    own_seg = lax.dynamic_slice_in_dim(segment_ids, shard_index * tok_rows, tok_rows)
    query_pos = shard_index * tok_rows + jnp.arange(tok_rows, dtype=jnp.int32)
    x_rows = tokens_in.astype(jnp.float32)
    normed_one, inv_one, ln_one = norm_forward(x_rows, gain_one, shift_one)
    ln_one_half = ln_one.astype(jnp.bfloat16)
    qkv_rows = back_product(ln_one_half, full_qkv) + jnp.concatenate(
        [q_bias, jnp.zeros_like(q_bias), v_bias]
    )
    queries = qkv_rows[:, :D].astype(jnp.bfloat16)
    kv_half = qkv_rows[:, D:].astype(jnp.bfloat16)
    kv_all = lax.all_gather(kv_half, "shard", axis=0, tiled=True)
    key_all = kv_all[:, :D]
    value_all = kv_all[:, D:]
    key_pos = jnp.arange(group_size, dtype=jnp.int32)
    allowed = (
        (own_seg[:, None] == segment_ids[None, :])
        & (key_pos[None, :] <= query_pos[:, None])
        & ((own_seg >= 0)[:, None] | (key_pos[None, :] == query_pos[:, None]))
    )
    attended, log_total = attend_forward(queries, key_all, value_all, allowed)
    resid = x_rows + back_product(attended, full_out) + out_bias
    normed_two, inv_two, ln_two = norm_forward(resid, gain_two, shift_two)
    ln_two_half = ln_two.astype(jnp.bfloat16)
    pre_act = back_product(ln_two_half, full_fc) + fc_bias
    act_half = jax.nn.gelu(pre_act, approximate=False).astype(jnp.bfloat16)
    act_parts = [act_half[:, t * D : (t + 1) * D] for t in range(n_shard)]
    out_sum = resid + proj_bias
    for act_part, proj_part in zip(act_parts, full_proj):
        out_sum = out_sum + back_product(act_part, proj_part)
    out_act = out_sum.astype(jnp.bfloat16)
    valid = (own_seg >= 0).astype(jnp.float32)
    grad_z = cotangent.astype(jnp.float32) * valid[:, None]
    gz_half = grad_z.astype(jnp.bfloat16)
    d_pre = jnp.concatenate([matmul(gz_half, part) for part in full_proj], axis=1) * gelu_slope(
        pre_act
    )
    gu_half = d_pre.astype(jnp.bfloat16)
    d_ln_two = matmul(gu_half, full_fc)
    d_resid = grad_z + norm_backward(d_ln_two, normed_two, inv_two, gain_two)
    gh_half = d_resid.astype(jnp.bfloat16)
    grad_attn = matmul(gh_half, full_out).astype(jnp.bfloat16)
    d_query, d_keys_all, d_values_all = attend_backward(
        queries, key_all, value_all, allowed, log_total, attended, grad_attn
    )
    d_kv = lax.psum_scatter(
        jnp.concatenate(
            [d_keys_all.astype(jnp.bfloat16), d_values_all.astype(jnp.bfloat16)], axis=1
        ),
        "shard",
        scatter_dimension=0,
        tiled=True,
    )
    d_values = d_kv[:, D:].astype(jnp.float32)
    gqkv_half = jnp.concatenate([d_query.astype(jnp.bfloat16), d_kv], axis=1)
    d_ln_one = matmul(gqkv_half, full_qkv)
    grad_input = (d_resid + norm_backward(d_ln_one, normed_one, inv_one, gain_one)).astype(
        jnp.bfloat16
    )
    small_rows = jnp.stack(
        [
            jnp.sum(d_ln_one * normed_one, axis=0),
            jnp.sum(d_ln_one, axis=0),
            jnp.sum(d_query, axis=0),
            jnp.sum(d_values, axis=0),
            jnp.sum(d_resid, axis=0),
            jnp.sum(d_ln_two * normed_two, axis=0),
            jnp.sum(d_ln_two, axis=0),
        ]
    )
    small_grad = jnp.concatenate(
        [small_rows, jnp.sum(d_pre, axis=0).reshape(4, D), jnp.sum(grad_z, axis=0)[None]], axis=0
    )
    small_send = jnp.swapaxes(
        pad_rows(small_grad.astype(jnp.bfloat16).astype(jnp.float32), eight(small_count)).reshape(
            -1, n_shard, rows_own
        ),
        0,
        1,
    )

    def weight_grad(left, right):
        return outer_sum(left, right).astype(jnp.bfloat16).reshape(n_dp, -1, unit, D)

    mixed = jnp.concatenate(
        [
            weight_grad(gqkv_half, ln_one_half),
            weight_grad(gh_half, attended),
            weight_grad(gu_half, ln_two_half),
        ],
        axis=1,
    ).reshape(n_dp, n_shard, PIECES - 1, unit, D)
    proj_grads = jnp.stack([weight_grad(gz_half, part) for part in act_parts], axis=1)
    swapped, proj_sum, small_sum = reduce_rows(
        jnp.concatenate([mixed, proj_grads], axis=2), small_send, n_dp, n_shard
    )
    mixed_sum = swapped.reshape(-1, rows_own).astype(jnp.float32)
    grad_qkv = mixed_sum[:cols_qkv].T
    grad_attn_out = mixed_sum[cols_qkv : cols_qkv + cols_out].T
    grad_fc = mixed_sum[cols_qkv + cols_out :].T
    grad_proj = proj_sum.astype(jnp.float32).T
    grad_small = small_sum[:small_count]
    upd_qkv = adam_update(w_qkv, moment_qkv, second_qkv, grad_qkv, WEIGHT_DECAY)
    upd_out = adam_update(w_attn_out, moment_attn_out, second_attn_out, grad_attn_out, WEIGHT_DECAY)
    upd_fc = adam_update(w_fc, moment_fc, second_fc, grad_fc, WEIGHT_DECAY)
    upd_proj = adam_update(w_proj, moment_proj, second_proj, grad_proj, WEIGHT_DECAY)
    upd_small = adam_update(small_w, moment_small, second_small, grad_small, 0.0)
    return (
        out_act,
        grad_input,
        grad_qkv,
        grad_attn_out,
        grad_fc,
        grad_proj,
        grad_small,
        upd_qkv[0],
        upd_out[0],
        upd_fc[0],
        upd_proj[0],
        upd_small[0],
        upd_qkv[1],
        upd_out[1],
        upd_fc[1],
        upd_proj[1],
        upd_small[1],
        upd_qkv[2],
        upd_out[2],
        upd_fc[2],
        upd_proj[2],
        upd_small[2],
    )


def solution(mesh):
    return jax.shard_map(
        on_device,
        mesh=mesh,
        in_specs=(
            P(("dp", "shard"), None),
            P(("dp", "shard"), None),
            P("dp"),
            P("shard", "dp"),
            P("shard", "dp"),
            P("shard", "dp"),
            P("shard", "dp"),
            P(None, "shard"),
            P("shard", "dp"),
            P("shard", "dp"),
            P("shard", "dp"),
            P("shard", "dp"),
            P(None, "shard"),
            P("shard", "dp"),
            P("shard", "dp"),
            P("shard", "dp"),
            P("shard", "dp"),
            P(None, "shard"),
        ),
        out_specs=(
            P(("dp", "shard"), None),
            P(("dp", "shard"), None),
            P("shard", "dp"),
            P("shard", "dp"),
            P("shard", "dp"),
            P("shard", "dp"),
            P(None, "shard"),
            P("shard", "dp"),
            P("shard", "dp"),
            P("shard", "dp"),
            P("shard", "dp"),
            P(None, "shard"),
            P("shard", "dp"),
            P("shard", "dp"),
            P("shard", "dp"),
            P("shard", "dp"),
            P(None, "shard"),
            P("shard", "dp"),
            P("shard", "dp"),
            P("shard", "dp"),
            P("shard", "dp"),
            P(None, "shard"),
        ),
        check_vma=False,
    )
```

```python
import math

import jax
import jax.numpy as jnp
from jax import lax
from jax.experimental import pallas as pl
from jax.experimental.pallas import tpu as pltpu
from jax.sharding import PartitionSpec as P

D = 1088
H = 17
HD = 64
FF = 4352
STEP = 3


NORM_EPS = 1e-05
LEARN_RATE = 0.01
BETA_ONE = 0.9
BETA_TWO = 0.95
ADAM_EPS = 1e-08
WEIGHT_DECAY = 0.1


def outer_sum(left_rows, right_rows):
    return lax.dot_general(
        left_rows, right_rows, (((0,), (0,)), ((), ())), preferred_element_type=jnp.float32
    )


def back_product(left_rows, right_rows):
    return lax.dot_general(
        left_rows, right_rows, (((1,), (1,)), ((), ())), preferred_element_type=jnp.float32
    )


def matmul(left_rows, right_rows):
    return jnp.dot(left_rows, right_rows, preferred_element_type=jnp.float32)


def norm_forward(row_data, gain_row, shift_row):
    row_mean = jnp.mean(row_data, axis=-1, keepdims=True)
    centered = row_data - row_mean
    variance = jnp.mean(centered * centered, axis=-1, keepdims=True)
    inverse_dev = lax.rsqrt(variance + NORM_EPS)
    normed = centered * inverse_dev
    return (normed, inverse_dev, normed * gain_row + shift_row)


def norm_backward(grad_rows, normed, inverse_dev, gain_row):
    scaled = grad_rows * gain_row
    return inverse_dev * (
        scaled
        - jnp.mean(scaled, axis=-1, keepdims=True)
        - normed * jnp.mean(scaled * normed, axis=-1, keepdims=True)
    )


def gelu_slope(pre_act):
    normal_cdf = 0.5 * (1.0 + lax.erf(pre_act * 0.7071067811865476))
    normal_pdf = jnp.exp(-0.5 * pre_act * pre_act) * 0.3989422804014327
    return normal_cdf + pre_act * normal_pdf


def head_split(rows_in):
    return rows_in.reshape(rows_in.shape[0], H, HD)


def prob_table(queries, key_rows, allowed, log_total):
    score_scale = 1.0 / math.sqrt(HD)
    scores = (
        jnp.einsum(
            "rhe,khe->hrk",
            head_split(queries),
            head_split(key_rows),
            preferred_element_type=jnp.float32,
        )
        * score_scale
    )
    if log_total is None:
        exp_scores = jnp.where(allowed[None], jnp.exp(scores), 0.0)
        log_total = jnp.log(jnp.sum(exp_scores, axis=-1))
    prob_full = jnp.where(allowed[None], jnp.exp(scores - log_total[..., None]), 0.0)
    return (prob_full, log_total)


def attend_forward(queries, key_rows, value_rows, allowed):
    prob_full, log_total = prob_table(queries, key_rows, allowed, None)
    prob_half = prob_full.astype(jnp.bfloat16)
    attended = jnp.einsum(
        "hrk,khe->rhe", prob_half, head_split(value_rows), preferred_element_type=jnp.float32
    )
    return (attended.reshape(queries.shape[0], H * HD).astype(jnp.bfloat16), log_total)


def attend_backward(queries, key_rows, value_rows, allowed, log_total, attended, grad_attn):
    row_count = queries.shape[0]
    key_count = key_rows.shape[0]
    score_scale = 1.0 / math.sqrt(HD)
    prob_full, unused_total = prob_table(queries, key_rows, allowed, log_total)
    prob_half = prob_full.astype(jnp.bfloat16)
    grad_heads = head_split(grad_attn)
    row_delta = jnp.sum(
        grad_heads.astype(jnp.float32) * head_split(attended).astype(jnp.float32), axis=-1
    )
    d_probs = jnp.einsum(
        "rhe,khe->hrk", grad_heads, head_split(value_rows), preferred_element_type=jnp.float32
    )
    d_scores = prob_full * (d_probs - jnp.transpose(row_delta)[..., None])
    grad_scores = (d_scores * score_scale).astype(jnp.bfloat16)
    d_query = jnp.einsum(
        "hrk,khe->rhe", grad_scores, head_split(key_rows), preferred_element_type=jnp.float32
    ).reshape(row_count, H * HD)
    d_keys = jnp.einsum(
        "hrk,rhe->khe", grad_scores, head_split(queries), preferred_element_type=jnp.float32
    ).reshape(key_count, H * HD)
    d_values = jnp.einsum(
        "hrk,rhe->khe", prob_half, grad_heads, preferred_element_type=jnp.float32
    ).reshape(key_count, H * HD)
    return (d_query, d_keys, d_values)


def adam_update(weight, moment_one, moment_two, gradient, decay_rate):
    moment_new = BETA_ONE * moment_one + (1.0 - BETA_ONE) * gradient
    second_new = BETA_TWO * moment_two + (1.0 - BETA_TWO) * gradient * gradient
    moment_hat = moment_new / (1.0 - BETA_ONE**STEP)
    second_hat = second_new / (1.0 - BETA_TWO**STEP)
    weight_new = weight - LEARN_RATE * (
        moment_hat / (jnp.sqrt(second_hat) + ADAM_EPS) + decay_rate * weight
    )
    return (weight_new, moment_new, second_new)


LANES = 128


def pad_rows(rows_in, count):
    return jnp.pad(rows_in, ((0, count - rows_in.shape[0]), (0, 0)))


def eight(count):
    return -(-count // 8) * 8


def tiles_of(piece):
    blocks = piece.shape[1] // LANES
    return jnp.concatenate(
        [piece[:, i * LANES : (i + 1) * LANES] for i in range(blocks)], axis=0
    )


def rest_rows(count, width):
    return -(-count // (LANES // width)) if width else 0


def rest_of(rest):
    count, width = rest.shape[-2:]
    fold = LANES // width
    rows = rest_rows(count, width)
    lead = rest.shape[:-2]
    rest = jnp.pad(rest, [(0, 0)] * len(lead) + [(0, fold * rows - count), (0, 0)])
    return jnp.swapaxes(rest.reshape(lead + (fold, rows, width)), -3, -2).reshape(
        lead + (rows, LANES)
    )


def rest_back(packed, count, width):
    fold = LANES // width
    lead, rows = packed.shape[:-2], packed.shape[-2]
    rest = jnp.swapaxes(packed.reshape(lead + (rows, fold, width)), -3, -2)
    return rest.reshape(lead + (fold * rows, width))[..., :count, :]


def by_shard(rows_in, parts):
    width = rows_in.shape[1] // parts
    main = width // LANES * LANES
    cuts = [rows_in[:, i * width : i * width + main] for i in range(parts)]
    cuts += [rows_in[:, i * width + main : (i + 1) * width] for i in range(parts)]
    return jnp.concatenate(cuts, axis=1)


def by_index(rows_in, parts):
    width = rows_in.shape[1] // parts
    main = width // LANES * LANES
    rest = width - main
    cuts = []
    for i in range(parts):
        cuts.append(rows_in[:, i * main : (i + 1) * main])
        cuts.append(rows_in[:, parts * main + i * rest : parts * main + (i + 1) * rest])
    return jnp.concatenate(cuts, axis=1)


def join_kernel(plan, tiles_ref, *refs):
    rest_refs, out_refs = refs[: len(plan)], refs[len(plan) :]
    for (start, count, blocks), rest_ref, out_ref in zip(plan, rest_refs, out_refs):
        parts = tiles_ref.shape[1]
        for i in range(parts):
            for j in range(blocks):
                lane = (i * blocks + j) * LANES
                out_ref[0, :, lane : lane + LANES] = tiles_ref[
                    0, i, start + j * count : start + (j + 1) * count, :
                ]
        out_ref[0, :, parts * blocks * LANES :] = rest_ref[0]


def join_tiles(gathered, plan, rests):
    n_dp, parts, rows, lanes = gathered.shape
    shapes = [
        (n_dp, count, parts * blocks * LANES + rest.shape[-1])
        for (start, count, blocks), rest in zip(plan, rests)
    ]
    return pl.pallas_call(
        lambda *refs: join_kernel(plan, *refs),
        grid=(n_dp,),
        in_specs=[pl.BlockSpec((1, parts, rows, lanes), lambda d: (d, 0, 0, 0))]
        + [pl.BlockSpec((1,) + rest.shape[1:], lambda d: (d, 0, 0)) for rest in rests],
        out_specs=[pl.BlockSpec((1,) + shape[1:], lambda d: (d, 0, 0)) for shape in shapes],
        out_shape=[jax.ShapeDtypeStruct(shape, gathered.dtype) for shape in shapes],
        compiler_params=pltpu.CompilerParams(vmem_limit_bytes=40 * 1024 * 1024),
    )(gathered, *rests)


def cut_kernel(plan, rest_starts, *refs):
    pairs = len(plan)
    left_refs, right_refs = refs[:pairs], refs[pairs : 2 * pairs]
    rest_refs, out_ref = refs[2 * pairs : -1], refs[-1]
    parts = out_ref.shape[1]
    for (start, count, blocks), left_ref, right_ref in zip(plan, left_refs, right_refs):
        for i in range(parts):
            width = blocks * LANES
            product = jnp.dot(
                left_ref[0],
                right_ref[:, i * width : (i + 1) * width],
                preferred_element_type=jnp.float32,
            ).astype(out_ref.dtype)
            for j in range(blocks):
                out_ref[0, i, start + j * count : start + (j + 1) * count, :] = product[
                    :, j * LANES : (j + 1) * LANES
                ]
    for start, rest_ref in zip(rest_starts, rest_refs):
        for i in range(parts):
            out_ref[0, i, start : start + rest_ref.shape[2], :] = rest_ref[0, i]


def cut_tiles(left_list, right_list, plan, rest_list, rest_starts, rows):
    n_dp, parts = rest_list[0].shape[:2]
    lefts = [
        left.T.reshape(n_dp, count, left.shape[0])
        for left, (start, count, blocks) in zip(left_list, plan)
    ]
    return pl.pallas_call(
        lambda *refs: cut_kernel(plan, rest_starts, *refs),
        grid=(n_dp,),
        in_specs=[pl.BlockSpec((1,) + left.shape[1:], lambda d: (d, 0, 0)) for left in lefts]
        + [pl.BlockSpec(right.shape, lambda d: (0, 0)) for right in right_list]
        + [pl.BlockSpec((1,) + rest.shape[1:], lambda d: (d, 0, 0, 0)) for rest in rest_list],
        out_specs=pl.BlockSpec((1, parts, rows, LANES), lambda d: (d, 0, 0, 0)),
        out_shape=jax.ShapeDtypeStruct((n_dp, parts, rows, LANES), jnp.bfloat16),
        compiler_params=pltpu.CompilerParams(vmem_limit_bytes=40 * 1024 * 1024),
    )(*lefts, *right_list, *rest_list)


def on_device_general(
    tokens_in,
    cotangent,
    segment_ids,
    w_qkv,
    w_attn_out,
    w_fc,
    w_proj,
    small_w,
    moment_qkv,
    moment_attn_out,
    moment_fc,
    moment_proj,
    moment_small,
    second_qkv,
    second_attn_out,
    second_fc,
    second_proj,
    second_small,
):
    axes = ("dp", "shard")
    n_dp = lax.axis_size("dp")
    n_shard = lax.axis_size("shard")
    rows_own, cols_qkv = w_qkv.shape
    cols_out = w_attn_out.shape[1]
    cols_fc = w_fc.shape[1]
    cols_proj = w_proj.shape[1]
    rows_proj = w_proj.shape[0]
    main_own = rows_own // LANES * LANES
    main_proj = rows_proj // LANES * LANES
    rest_own, rest_proj = rows_own - main_own, rows_proj - main_proj
    col_list = (cols_qkv, cols_out, cols_fc)
    col_sum = sum(col_list)
    sizes = [count * (main_own // LANES) for count in col_list]
    sizes += [cols_proj * (main_proj // LANES)]
    sizes += [eight(rest_rows(col_sum, rest_own)), eight(rest_rows(cols_proj, rest_proj))]
    starts = [sum(sizes[:i]) for i in range(len(sizes) + 1)]
    pieces = [w.astype(jnp.bfloat16).T for w in (w_qkv, w_attn_out, w_fc)]
    piece_proj = w_proj.astype(jnp.bfloat16).T
    rest_one = jnp.concatenate([piece[:, main_own:] for piece in pieces], axis=0)
    small_count = small_w.shape[0] * rows_own
    small_tiles = eight(-(-small_count // LANES))
    small_flat = jnp.pad(
        small_w.astype(jnp.bfloat16).reshape(small_count), (0, small_tiles * LANES - small_count)
    )
    packed = jnp.concatenate(
        [tiles_of(piece[:, :main_own]) for piece in pieces]
        + [
            tiles_of(piece_proj[:, :main_proj]),
            pad_rows(rest_of(rest_one), sizes[4]),
            pad_rows(rest_of(piece_proj[:, main_proj:]), sizes[5]),
            small_flat.reshape(small_tiles, LANES),
        ],
        axis=0,
    )
    gathered = lax.all_gather(packed, axes, axis=0, tiled=False).reshape(
        n_dp, n_shard, packed.shape[0], LANES
    )

    def rows_at(start, count):
        return lax.slice_in_dim(gathered, start, start + count, axis=2)

    all_rest = jnp.swapaxes(
        rest_back(rows_at(starts[4], rest_rows(col_sum, rest_own)), col_sum, rest_own), 1, 2
    ).reshape(n_dp, col_sum, n_shard * rest_own)

    proj_rest = jnp.swapaxes(
        rest_back(rows_at(starts[5], rest_rows(cols_proj, rest_proj)), cols_proj, rest_proj), 1, 2
    ).reshape(n_dp, cols_proj, n_shard * rest_proj)
    own_blocks = main_own // LANES
    plan = [
        (starts[0], cols_qkv, own_blocks),
        (starts[1], cols_out, own_blocks),
        (starts[2], cols_fc, own_blocks),
        (starts[3], cols_proj, main_proj // LANES),
    ]
    rests = [
        all_rest[:, :cols_qkv],
        all_rest[:, cols_qkv : cols_qkv + cols_out],
        all_rest[:, cols_qkv + cols_out :],
        proj_rest,
    ]
    full_qkv, full_out, full_fc, full_proj = (
        full.reshape(full.shape[0] * full.shape[1], full.shape[2])
        for full in join_tiles(gathered, plan, rests)
    )
    full_small = jnp.transpose(
        gathered[0, :, starts[6] :]
        .reshape(n_shard, small_tiles * LANES)[:, :small_count]
        .reshape(n_shard, small_w.shape[0], rows_own),
        (1, 0, 2),
    ).reshape(small_w.shape[0], n_shard * rows_own)
    small_vals = full_small.astype(jnp.float32)
    gain_one = small_vals[0]
    shift_one = small_vals[1]
    q_bias = small_vals[2]
    v_bias = small_vals[3]
    out_bias = small_vals[4]
    gain_two = small_vals[5]
    shift_two = small_vals[6]
    fc_bias = small_vals[7:11].reshape(FF)
    proj_bias = small_vals[11]
    tok_rows = tokens_in.shape[0]
    group_size = segment_ids.shape[0]
    shard_index = lax.axis_index("shard")
    own_seg = lax.dynamic_slice_in_dim(segment_ids, shard_index * tok_rows, tok_rows)
    query_pos = shard_index * tok_rows + jnp.arange(tok_rows, dtype=jnp.int32)
    x_rows = tokens_in.astype(jnp.float32)
    normed_one, inv_one, ln_one = norm_forward(x_rows, gain_one, shift_one)
    ln_one_half = ln_one.astype(jnp.bfloat16)
    ln_one_cut = by_shard(ln_one_half, n_shard)
    qkv_rows = back_product(ln_one_cut, full_qkv) + jnp.concatenate(
        [q_bias, jnp.zeros_like(q_bias), v_bias]
    )
    queries = qkv_rows[:, :D].astype(jnp.bfloat16)
    kv_half = qkv_rows[:, D:].astype(jnp.bfloat16)
    kv_all = lax.all_gather(kv_half, "shard", axis=0, tiled=True)
    key_all = kv_all[:, :D]
    value_all = kv_all[:, D:]
    key_pos = jnp.arange(group_size, dtype=jnp.int32)
    allowed = (
        (own_seg[:, None] == segment_ids[None, :])
        & (key_pos[None, :] <= query_pos[:, None])
        & ((own_seg >= 0)[:, None] | (key_pos[None, :] == query_pos[:, None]))
    )
    attended, log_total = attend_forward(queries, key_all, value_all, allowed)
    attended_cut = by_shard(attended, n_shard)
    resid = x_rows + back_product(attended_cut, full_out) + out_bias
    normed_two, inv_two, ln_two = norm_forward(resid, gain_two, shift_two)
    ln_two_half = ln_two.astype(jnp.bfloat16)
    ln_two_cut = by_shard(ln_two_half, n_shard)
    pre_act = back_product(ln_two_cut, full_fc) + fc_bias
    act_half = jax.nn.gelu(pre_act, approximate=False).astype(jnp.bfloat16)
    act_cut = by_shard(act_half, n_shard)
    out_act = (resid + back_product(act_cut, full_proj) + proj_bias).astype(jnp.bfloat16)
    valid = (own_seg >= 0).astype(jnp.float32)
    grad_z = cotangent.astype(jnp.float32) * valid[:, None]
    gz_half = grad_z.astype(jnp.bfloat16)
    d_pre = by_index(matmul(gz_half, full_proj), n_shard) * gelu_slope(pre_act)
    gu_half = d_pre.astype(jnp.bfloat16)
    d_ln_two = by_index(matmul(gu_half, full_fc), n_shard)
    d_resid = grad_z + norm_backward(d_ln_two, normed_two, inv_two, gain_two)
    gh_half = d_resid.astype(jnp.bfloat16)
    grad_attn = by_index(matmul(gh_half, full_out).astype(jnp.bfloat16), n_shard)
    d_query, d_keys_all, d_values_all = attend_backward(
        queries, key_all, value_all, allowed, log_total, attended, grad_attn
    )
    d_kv = lax.psum_scatter(
        jnp.concatenate(
            [d_keys_all.astype(jnp.bfloat16), d_values_all.astype(jnp.bfloat16)], axis=1
        ),
        "shard",
        scatter_dimension=0,
        tiled=True,
    )
    d_values = d_kv[:, D:].astype(jnp.float32)
    gqkv_half = jnp.concatenate([d_query.astype(jnp.bfloat16), d_kv], axis=1)
    d_ln_one = by_index(matmul(gqkv_half, full_qkv), n_shard)
    grad_input = (d_resid + norm_backward(d_ln_one, normed_one, inv_one, gain_one)).astype(
        jnp.bfloat16
    )
    small_rows = jnp.stack(
        [
            jnp.sum(d_ln_one * normed_one, axis=0),
            jnp.sum(d_ln_one, axis=0),
            jnp.sum(d_query, axis=0),
            jnp.sum(d_values, axis=0),
            jnp.sum(d_resid, axis=0),
            jnp.sum(d_ln_two * normed_two, axis=0),
            jnp.sum(d_ln_two, axis=0),
        ]
    )
    small_grad = jnp.concatenate(
        [small_rows, jnp.sum(d_pre, axis=0).reshape(4, D), jnp.sum(grad_z, axis=0)[None]], axis=0
    )
    lefts = (gqkv_half, gh_half, gu_half, gz_half)
    rights = (ln_one_cut, attended_cut, ln_two_cut, act_cut)

    def rest_cut(left, right, main, rest):
        product = outer_sum(left, right[:, n_shard * main :]).astype(jnp.bfloat16)
        count = product.shape[0] // n_dp
        return jnp.swapaxes(product.reshape(n_dp, count, n_shard, rest), 1, 2)

    def fill(packed_rest, count):
        return jnp.pad(
            packed_rest, ((0, 0), (0, 0), (0, count - packed_rest.shape[2]), (0, 0))
        )

    outgoing = cut_tiles(
        lefts,
        rights,
        plan,
        [
            fill(
                rest_of(
                    jnp.concatenate(
                        [
                            rest_cut(left, right, main_own, rest_own)
                            for left, right in zip(lefts[:3], rights[:3])
                        ],
                        axis=2,
                    )
                ),
                sizes[4],
            ),
            fill(rest_of(rest_cut(gz_half, act_cut, main_proj, rest_proj)), sizes[5]),
        ],
        starts[4:6],
        starts[6],
    ).reshape(n_dp * n_shard, starts[6], LANES)
    summed = lax.psum_scatter(outgoing, axes, scatter_dimension=0, tiled=False).astype(
        jnp.float32
    )

    def owned(start, count, main, rest):
        blocks = main // LANES
        cuts = [summed[start + i * count : start + (i + 1) * count] for i in range(blocks)]
        return jnp.concatenate(cuts + [rest], axis=1).T

    sum_rest = rest_back(
        summed[starts[4] : starts[4] + rest_rows(col_sum, rest_own)], col_sum, rest_own
    )
    grad_qkv = owned(starts[0], cols_qkv, main_own, sum_rest[:cols_qkv])
    grad_attn_out = owned(
        starts[1], cols_out, main_own, sum_rest[cols_qkv : cols_qkv + cols_out]
    )
    grad_fc = owned(starts[2], cols_fc, main_own, sum_rest[cols_qkv + cols_out :])
    grad_proj = owned(
        starts[3],
        cols_proj,
        main_proj,
        rest_back(
            summed[starts[5] : starts[5] + rest_rows(cols_proj, rest_proj)], cols_proj, rest_proj
        ),
    )
    small_total = lax.psum(small_grad.astype(jnp.bfloat16).astype(jnp.float32), axes)
    grad_small = lax.dynamic_slice_in_dim(
        small_total, shard_index * rows_own, rows_own, axis=1
    )
    upd_qkv = adam_update(w_qkv, moment_qkv, second_qkv, grad_qkv, WEIGHT_DECAY)
    upd_out = adam_update(w_attn_out, moment_attn_out, second_attn_out, grad_attn_out, WEIGHT_DECAY)
    upd_fc = adam_update(w_fc, moment_fc, second_fc, grad_fc, WEIGHT_DECAY)
    upd_proj = adam_update(w_proj, moment_proj, second_proj, grad_proj, WEIGHT_DECAY)
    upd_small = adam_update(small_w, moment_small, second_small, grad_small, 0.0)
    return (
        out_act,
        grad_input,
        grad_qkv,
        grad_attn_out,
        grad_fc,
        grad_proj,
        grad_small,
        upd_qkv[0],
        upd_out[0],
        upd_fc[0],
        upd_proj[0],
        upd_small[0],
        upd_qkv[1],
        upd_out[1],
        upd_fc[1],
        upd_proj[1],
        upd_small[1],
        upd_qkv[2],
        upd_out[2],
        upd_fc[2],
        upd_proj[2],
        upd_small[2],
    )


AXES = ("dp", "shard")
MESH_ID = pl.DeviceIdType.MESH
COLS = 2
PIECES = 3
SLOTS = 4


def place():
    d = lax.axis_index("dp")
    s = lax.axis_index("shard")
    z, y = d // COLS, d % COLS
    x, c = s // 2, s % 2
    x_dev = (d, (1 - x) * 2 + c)
    y_dev = (z * COLS + 1 - y, s)
    near = tuple(a * (1 - c) + b * c for a, b in zip(x_dev, y_dev))
    far = tuple(b * (1 - c) + a * c for a, b in zip(x_dev, y_dev))
    up = (d + COLS, s)
    down = (d - COLS, s)
    sib = (d, x * 2 + 1 - c)
    return d, s, z, y, x, c, near, far, up, down, sib


def flip(value, change):
    return value + change - 2 * value * change


def enter(n_dp, n_shard, d, s):
    barrier = pltpu.get_barrier_semaphore()
    for step in range(1, n_dp):
        pl.semaphore_signal(
            barrier, inc=1, device_id=((d + step) % n_dp, s), device_id_type=MESH_ID
        )
    for step in range(1, n_shard):
        pl.semaphore_signal(
            barrier, inc=1, device_id=(d, (s + step) % n_shard), device_id_type=MESH_ID
        )
    pl.semaphore_wait(barrier, n_dp + n_shard - 2)


def gather_kernel(
    n_dp,
    n_shard,
    cut_ref,
    proj_ref,
    small_ref,
    full_ref,
    small_out,
    own,
    swap,
    local_sem,
    swap_sem,
    small_sem,
    send_sem,
    recv_sem,
    sib_sem,
):
    d, s, z, y, x, c, near, far, up, down, sib = place()
    depth = n_dp // COLS
    lanes = cut_ref.shape[-1]

    def where(zs, fa, fb):
        fx = fa * (1 - c) + fb * c
        fy = fb * (1 - c) + fa * c
        return zs * COLS + flip(y, fy), flip(x, fx) * 2 + c

    def number(zs, fa, fb, k):
        return ((zs * 2 + fa) * 2 + fb) * PIECES + k

    def copy(kind, zs, fa, fb, k, src=None):
        dp, sh = where(zs, fa, fb)
        block = full_ref.at[dp, sh, k]
        target = (near, far, up, down, sib)[kind]
        mine = number(zs, fa, fb, k)
        if kind == 4:
            arrive = sib_sem.at[mine]
        else:
            arrive = recv_sem.at[number(zs, 1 if kind == 0 else fa, 1 if kind == 1 else fb, k)]
        return pltpu.make_async_remote_copy(
            src_ref=block if src is None else src,
            dst_ref=block,
            send_sem=send_sem.at[kind, mine],
            recv_sem=arrive,
            device_id=target,
            device_id_type=MESH_ID,
        )

    def arrived(zs, fa, fb, k):
        dp, sh = where(zs, fa, fb)
        block = full_ref.at[dp, sh, k]
        pltpu.make_async_copy(block, block, recv_sem.at[number(zs, fa, fb, k)]).wait()

    enter(n_dp, n_shard, d, s)

    def swap_copy(step):
        peer = (s + step) % n_shard
        return pltpu.make_async_remote_copy(
            src_ref=cut_ref.at[peer],
            dst_ref=swap.at[s],
            send_sem=swap_sem.at[0, step],
            recv_sem=swap_sem.at[1, step],
            device_id=(d, peer),
            device_id_type=MESH_ID,
        )

    def small_copy(step):
        peer = (s + step) % n_shard
        return pltpu.make_async_remote_copy(
            src_ref=small_ref,
            dst_ref=small_out.at[s],
            send_sem=small_sem.at[0, step],
            recv_sem=small_sem.at[1, step],
            device_id=(d, peer),
            device_id_type=MESH_ID,
        )

    for step in range(1, n_shard):
        swap_copy(step).start()
    own_cut = pltpu.make_async_copy(cut_ref.at[s], swap.at[s], local_sem.at[0])
    own_cut.start()
    own_small = pltpu.make_async_copy(small_ref, small_out.at[s], local_sem.at[1])
    own_small.start()

    def spread(k, src):
        copy(0, z, 0, 0, k, src).start()
        copy(1, z, 0, 0, k, src).start()

        @pl.when(z < depth - 1)
        def _():
            copy(2, z, 0, 0, k, src).start()

        @pl.when(z > 0)
        def _():
            copy(3, z, 0, 0, k, src).start()

        copy(4, z, 0, 0, k, src).start()
        keep = pltpu.make_async_copy(src, full_ref.at[d, s, k], local_sem.at[2 + k])
        keep.start()

    spread(2, proj_ref)
    for step in range(1, n_shard):
        small_copy(step).start()
    own_cut.wait()
    for step in range(1, n_shard):
        swap_copy(step).wait()
    for k in (1, 0):
        for part in range(n_shard):
            own[k, :, part * lanes : (part + 1) * lanes] = swap[part, k]
    spread(1, own.at[1])
    spread(0, own.at[0])

    def pass_on(zs, fa, k, go_up, go_down, go_near):
        arrived(zs, fa, 0, k)
        if go_up:

            @pl.when(z < depth - 1)
            def _():
                copy(2, zs, fa, 0, k).start()

        if go_down:

            @pl.when(z > 0)
            def _():
                copy(3, zs, fa, 0, k).start()

        if go_near:
            copy(0, zs, fa, 0, k).start()
        copy(1, zs, fa, 0, k).start()
        copy(4, zs, fa, 0, k).start()

    def from_near(zs):
        for k in (1, 0):
            pass_on(zs, 1, k, False, False, False)

    def from_far(zs):
        def step(j, carry):
            fa, k = j % 2, PIECES - 1 - j // 2
            arrived(zs, fa, 1, k)
            copy(4, zs, fa, 1, k).start()
            return carry

        lax.fori_loop(0, 2 * PIECES, step, 0)

    pass_on(z, 1, 2, True, True, False)
    from_near(z)
    for delta in range(1, depth):
        for sign in (-1, 1):
            zs = z + sign * delta

            @pl.when((zs >= 0) & (zs < depth))
            def _():
                for k, fa in ((2, 0), (2, 1), (1, 0), (0, 0)):
                    pass_on(zs, fa, k, sign < 0, sign > 0, k < 2)

        for sign in (-1, 1):
            zs = z + sign * delta

            @pl.when((zs >= 0) & (zs < depth))
            def _():
                from_near(zs)

        for sign in (-1, 1) if delta > 1 else (0,):
            zs = z + sign * (delta - 1)

            @pl.when((zs >= 0) & (zs < depth))
            def _():
                from_far(zs)

    for sign in (-1, 1):
        zs = z + sign * (depth - 1)

        @pl.when((zs >= 0) & (zs < depth))
        def _():
            from_far(zs)

    own_small.wait()
    for k in range(PIECES):
        pltpu.make_async_copy(own.at[0], full_ref.at[d, s, k], local_sem.at[2 + k]).wait()
    for step in range(1, n_shard):
        small_copy(step).wait()

    def finish(zs, carry):
        for fa in range(2):
            for k in range(PIECES):
                if k == 2 or fa == 0:

                    @pl.when((z < depth - 1) & (zs <= z))
                    def _():
                        copy(2, zs, fa, 0, k).wait_send()

                    @pl.when((z > 0) & (zs >= z))
                    def _():
                        copy(3, zs, fa, 0, k).wait_send()

                if fa == 0:
                    if k < 2:
                        copy(0, zs, fa, 0, k).wait_send()
                    else:

                        @pl.when(zs == z)
                        def _():
                            copy(0, zs, fa, 0, k).wait_send()

                copy(1, zs, fa, 0, k).wait_send()
                for fb in range(2):
                    copy(4, zs, fa, fb, k).wait()
        return carry

    lax.fori_loop(0, depth, finish, 0)


def gather_rows(cut, proj, small, n_dp, n_shard):
    piece_rows, width = proj.shape
    count = n_dp // COLS * 4 * PIECES
    shape = (n_dp, n_shard, PIECES, piece_rows, width)
    return pl.pallas_call(
        lambda *refs: gather_kernel(n_dp, n_shard, *refs),
        out_shape=[
            jax.ShapeDtypeStruct(shape, cut.dtype),
            jax.ShapeDtypeStruct((n_shard,) + small.shape, small.dtype),
        ],
        in_specs=[pl.BlockSpec(memory_space=pltpu.VMEM)] * 3,
        out_specs=[
            pl.BlockSpec(memory_space=pltpu.HBM),
            pl.BlockSpec(memory_space=pltpu.VMEM),
        ],
        scratch_shapes=[
            pltpu.VMEM((PIECES - 1, piece_rows, width), cut.dtype),
            pltpu.VMEM(cut.shape, cut.dtype),
            pltpu.SemaphoreType.DMA((2 + PIECES,)),
            pltpu.SemaphoreType.DMA((2, n_shard)),
            pltpu.SemaphoreType.DMA((2, n_shard)),
            pltpu.SemaphoreType.DMA((5, count)),
            pltpu.SemaphoreType.DMA((count,)),
            pltpu.SemaphoreType.DMA((count,)),
        ],
        compiler_params=pltpu.CompilerParams(
            collective_id=0, has_side_effects=True, vmem_limit_bytes=60 * 1024 * 1024
        ),
    )(cut, proj, small)


def reduce_kernel(
    n_dp,
    n_shard,
    grad_ref,
    small_ref,
    swap_out,
    proj_out,
    small_out,
    total,
    from_sib,
    from_far,
    from_near,
    from_line,
    cut,
    small_part,
    small_sum,
    small_all,
    local_sem,
    sib_sem,
    far_sem,
    near_sem,
    line_sem,
    swap_sem,
    small_sem,
    small_dp_sem,
    own_sem,
):
    d, s, z, y, x, c, near, far, up, down, sib = place()
    depth = n_dp // COLS
    lanes = swap_out.shape[-1]
    per_level = 2 * PIECES

    def where(zq, fa, fb, core):
        fx = fa * (1 - core) + fb * core
        fy = fb * (1 - core) + fa * core
        return zq * COLS + flip(y, fy), flip(x, fx) * 2 + core

    def spot(zq, fa, fb, k):
        return ((zq * 2 + fb) * 2 + fa) * PIECES + k

    def order(j):
        level = j // per_level
        zq = (level % 2) * (depth - 1 - level // 2) + (1 - level % 2) * (level // 2)
        k = j % per_level // 2
        fa = 1 - j % 2
        return zq, fa, k

    def remote(src, dst, sems, number, target):
        return pltpu.make_async_remote_copy(
            src_ref=src,
            dst_ref=dst,
            send_sem=sems.at[0, number],
            recv_sem=sems.at[1, number],
            device_id=target,
            device_id_type=MESH_ID,
        )

    def sib_copy(zq, fa, fb, k):
        dp, sh = where(zq, fa, fb, 1 - c)
        slot = spot(zq, fa, fb, k)
        return remote(grad_ref.at[dp, sh, k], from_sib.at[slot], sib_sem, slot, sib)

    def own_copy(zq, fa, fb, k):
        dp, sh = where(zq, fa, fb, c)
        slot = spot(zq, fa, fb, k)
        return pltpu.make_async_copy(grad_ref.at[dp, sh, k], total.at[slot], local_sem.at[slot])

    def far_copy(zq, fa, k):
        slot = (zq * 2 + fa) * PIECES + k
        return remote(total.at[spot(zq, fa, 1, k)], from_far.at[slot], far_sem, slot, far)

    def near_copy(zq, k, slot):
        return remote(total.at[spot(zq, 1, 0, k)], from_near.at[slot], near_sem, slot, near)

    def line_copy(way, zq, fa, k):
        slot = (way * depth + zq) * SLOTS + k + fa
        return remote(
            total.at[spot(zq, fa, 0, k)],
            from_line.at[slot],
            line_sem,
            slot,
            (up, down)[way],
        )

    def add(slot, other):
        total[slot] = (
            total[slot].astype(jnp.float32) + other[...].astype(jnp.float32)
        ).astype(total.dtype)

    enter(n_dp, n_shard, d, s)

    def small_shard(step):
        peer = (s + step) % n_shard
        return remote(small_ref.at[peer], small_part.at[s], small_sem, step, (d, peer))

    for step in range(1, n_shard):
        small_shard(step).start()
    own_small = pltpu.make_async_copy(small_ref.at[s], small_part.at[s], own_sem.at[0])
    own_small.start()

    def begin(fb):
        def step(j, carry):
            zq, fa, k = order(j)
            sib_copy(zq, fa, fb, k).start()
            own_copy(zq, fa, fb, k).start()
            return carry

        return step

    lax.fori_loop(0, depth * per_level, begin(1), 0)
    lax.fori_loop(0, depth * per_level, begin(0), 0)

    def merge(fb):
        def step(j, carry):
            zq, fa, k = order(j)
            own_copy(zq, fa, fb, k).wait()
            sib_copy(zq, fa, fb, k).wait_recv()
            slot = spot(zq, fa, fb, k)
            add(slot, from_sib.at[slot])
            if fb == 1:
                far_copy(zq, fa, k).start()
            return carry

        return step

    lax.fori_loop(0, depth * per_level, merge(1), 0)

    own_small.wait()
    for step in range(1, n_shard):
        small_shard(step).wait()
    small_sum[...] = jnp.sum(small_part[...], axis=0)

    def small_dp(step):
        peer = (d + step) % n_dp
        return remote(small_sum, small_all.at[d], small_dp_sem, step, (peer, s))

    lax.fori_loop(0, depth * per_level, merge(0), 0)
    for step in range(1, n_dp):
        small_dp(step).start()
    own_all = pltpu.make_async_copy(small_sum, small_all.at[d], own_sem.at[1])
    own_all.start()

    def level_step(level, carry):
        zq = (level % 2) * (depth - 1 - level // 2) + (1 - level % 2) * (level // 2)

        def line_step(fa, k):
            @pl.when(zq < z)
            def _():
                @pl.when(z < depth - 1)
                def _():
                    line_copy(1, zq, fa, k).wait_recv()
                    add(spot(zq, fa, 0, k), from_line.at[(depth + zq) * SLOTS + k + fa])

                line_copy(1, zq, fa, k).start()

            @pl.when(zq > z)
            def _():
                @pl.when(z > 0)
                def _():
                    line_copy(0, zq, fa, k).wait_recv()
                    add(spot(zq, fa, 0, k), from_line.at[zq * SLOTS + k + fa])

                line_copy(0, zq, fa, k).start()

        def take_far(fa, k):
            far_copy(zq, fa, k).wait_recv()
            add(spot(zq, fa, 0, k), from_far.at[(zq * 2 + fa) * PIECES + k])

        for k in (0, 1):
            take_far(1, k)
            near_copy(zq, k, k * depth + zq).start()
            take_far(0, k)
        for fa in (1, 0):
            take_far(fa, 2)
            line_step(fa, 2)
        for k in (0, 1):
            near_copy(zq, k, k * depth + zq).wait_recv()
            add(spot(zq, 0, 0, k), from_near.at[k * depth + zq])
            line_step(0, k)
        return carry

    lax.fori_loop(0, depth, level_step, 0)

    def last(fa, k):
        number = k + fa

        @pl.when(z < depth - 1)
        def _():
            line_copy(1, z, fa, k).wait_recv()
            add(spot(z, fa, 0, k), from_line.at[(depth + z) * SLOTS + number])

        @pl.when(z > 0)
        def _():
            line_copy(0, z, fa, k).wait_recv()
            add(spot(z, fa, 0, k), from_line.at[z * SLOTS + number])

    last(1, 2)
    near_copy(z, 2, 2 * depth).start()
    for k in (0, 1):
        last(0, k)
        for part in range(n_shard):
            cut[part, k] = total[spot(z, 0, 0, k), :, part * lanes : (part + 1) * lanes]

    def swap_copy(step):
        peer = (s + step) % n_shard
        return remote(cut.at[peer], swap_out.at[s], swap_sem, step, (d, peer))

    for step in range(1, n_shard):
        swap_copy(step).start()
    own_cut = pltpu.make_async_copy(cut.at[s], swap_out.at[s], own_sem.at[2])
    own_cut.start()
    last(0, 2)
    near_copy(z, 2, 2 * depth).wait_recv()
    add(spot(z, 0, 0, 2), from_near.at[2 * depth])
    proj_out[...] = total[spot(z, 0, 0, 2)]
    own_all.wait()
    for step in range(1, n_dp):
        small_dp(step).wait()
    small_out[...] = jnp.sum(small_all[...], axis=0)
    own_cut.wait()
    for step in range(1, n_shard):
        swap_copy(step).wait()

    def finish(zq, carry):
        for k in range(PIECES):
            for fa in range(2):
                for fb in range(2):
                    sib_copy(zq, fa, fb, k).wait_send()
                far_copy(zq, fa, k).wait_send()
                if k == 2 or fa == 0:

                    @pl.when(zq < z)
                    def _():
                        line_copy(1, zq, fa, k).wait_send()

                    @pl.when(zq > z)
                    def _():
                        line_copy(0, zq, fa, k).wait_send()

        for k in (0, 1):
            near_copy(zq, k, k * depth + zq).wait_send()
        return carry

    lax.fori_loop(0, depth, finish, 0)
    near_copy(z, 2, 2 * depth).wait_send()


def reduce_rows(grads, small, n_dp, n_shard):
    piece_rows, width = grads.shape[-2:]
    lanes = width // n_shard
    depth = n_dp // COLS
    count = depth * 4 * PIECES
    kind = grads.dtype

    def pieces(number):
        return pltpu.VMEM((number, piece_rows, width), kind)

    def sems(*shape):
        return pltpu.SemaphoreType.DMA(shape)

    return pl.pallas_call(
        lambda *refs: reduce_kernel(n_dp, n_shard, *refs),
        out_shape=[
            jax.ShapeDtypeStruct((n_shard, PIECES - 1, piece_rows, lanes), kind),
            jax.ShapeDtypeStruct((piece_rows, width), kind),
            jax.ShapeDtypeStruct(small.shape[1:], small.dtype),
        ],
        in_specs=[
            pl.BlockSpec(memory_space=pltpu.HBM),
            pl.BlockSpec(memory_space=pltpu.VMEM),
        ],
        out_specs=[pl.BlockSpec(memory_space=pltpu.VMEM)] * 3,
        scratch_shapes=[
            pieces(count),
            pieces(count),
            pieces(depth * 2 * PIECES),
            pieces(2 * depth + 1),
            pieces(2 * depth * SLOTS),
            pltpu.VMEM((n_shard, PIECES - 1, piece_rows, lanes), kind),
            pltpu.VMEM(small.shape, small.dtype),
            pltpu.VMEM(small.shape[1:], small.dtype),
            pltpu.VMEM((n_dp,) + small.shape[1:], small.dtype),
            sems(count),
            sems(2, count),
            sems(2, depth * 2 * PIECES),
            sems(2, 2 * depth + 1),
            sems(2, 2 * depth * SLOTS),
            sems(2, n_shard),
            sems(2, n_shard),
            sems(2, n_dp),
            sems(3),
        ],
        compiler_params=pltpu.CompilerParams(
            collective_id=1, has_side_effects=True, vmem_limit_bytes=62 * 1024 * 1024
        ),
    )(grads, small)


def block_specs(blocks, unit, width):
    specs = []
    for t_start, t_count, k_start, k_count in blocks:
        specs.append(
            pl.BlockSpec(
                (1, t_count, k_count, unit, width),
                lambda d, t=t_start // t_count, k=k_start // k_count: (d, t, k, 0, 0),
            )
        )
    return specs


def block_units(refs, blocks):
    return [
        ref[0, t, k]
        for ref, (t_start, t_count, k_start, k_count) in zip(refs, blocks)
        for t in range(t_count)
        for k in range(k_count)
    ]


def block_cost(count, full, rows):
    elements = count * full.shape[0] * full.shape[3] * full.shape[4]
    return pl.CostEstimate(
        flops=2 * elements * rows, bytes_accessed=2 * elements, transcendentals=0
    )


QKV_BLOCKS = ((0, 1, 0, 2), (1, 1, 0, 1))
OUT_BLOCKS = ((1, 1, 1, 1),)
FC_BLOCKS = ((2, 2, 0, 2),)
PROJ_BLOCKS = ((0, 4, 2, 1),)


def forward_product(rows_in, full, blocks):
    n_dp, unit, width = full.shape[0], full.shape[3], full.shape[4]
    summed = rows_in.ndim == 3
    count = sum(b[1] * b[3] for b in blocks)
    rows = rows_in.shape[-2]
    out_count = 1 if summed else count

    def kernel(rows_ref, *refs):
        out_ref = refs[-1]
        total = None
        for i, block in enumerate(block_units(refs[:-1], blocks)):
            left = rows_ref[i] if summed else rows_ref[...]
            product = back_product(block, left)
            if summed:
                total = product if total is None else total + product
            else:
                out_ref[0, i] = product
        if summed:
            out_ref[0, 0] = total

    out = pl.pallas_call(
        kernel,
        grid=(n_dp,),
        in_specs=[pl.BlockSpec(rows_in.shape, lambda d: (0,) * rows_in.ndim)]
        + block_specs(blocks, unit, width),
        out_specs=pl.BlockSpec((1, out_count, unit, rows), lambda d: (d, 0, 0, 0)),
        out_shape=jax.ShapeDtypeStruct((n_dp, out_count, unit, rows), jnp.float32),
        compiler_params=pltpu.CompilerParams(vmem_limit_bytes=32 * 1024 * 1024),
        cost_estimate=block_cost(count, full, rows),
    )(rows_in, *[full] * len(blocks))
    return out.reshape(n_dp * out_count * unit, rows).T


def backward_product(left, full, blocks):
    n_dp, unit, width = full.shape[0], full.shape[3], full.shape[4]
    count = sum(b[1] * b[3] for b in blocks)
    rows = left.shape[-1]
    summed = left.shape[1] == count
    out_count = 1 if summed else count

    def kernel(left_ref, *refs):
        out_ref = refs[-1]
        products = []
        for i, block in enumerate(block_units(refs[:-1], blocks)):
            products.append(outer_sum(left_ref[0, i if summed else 0], block))
        if summed:
            products = [sum(products[1:], products[0])]
        first = pl.program_id(0) == 0

        @pl.when(first)
        def _():
            for i, product in enumerate(products):
                out_ref[i] = product

        @pl.when(jnp.logical_not(first))
        def _():
            for i, product in enumerate(products):
                out_ref[i] += product

    out = pl.pallas_call(
        kernel,
        grid=(n_dp,),
        in_specs=[pl.BlockSpec((1,) + left.shape[1:], lambda d: (d, 0, 0, 0))]
        + block_specs(blocks, unit, width),
        out_specs=pl.BlockSpec((out_count, rows, width), lambda d: (0, 0, 0)),
        out_shape=jax.ShapeDtypeStruct((out_count, rows, width), jnp.float32),
        compiler_params=pltpu.CompilerParams(vmem_limit_bytes=40 * 1024 * 1024),
        cost_estimate=block_cost(count, full, rows),
    )(left, *[full] * len(blocks))
    return out[0] if summed else out


def per_dp(array):
    return pl.BlockSpec((1,) + array.shape[1:], lambda d: (d,) + (0,) * (array.ndim - 1))


def whole(array):
    return pl.BlockSpec(array.shape, lambda d: (0,) * array.ndim)


def late_grads(fc_units, proj_units, fc_rows, act_parts, n_shard):
    n_dp, _, unit, rows = proj_units.shape
    width = fc_rows.shape[-1]

    def kernel(fc_ref, proj_ref, rows_ref, act_ref, out_ref):
        for i in range(4):
            out_ref[0, 2 + i // 2, i % 2] = matmul(fc_ref[0, i], rows_ref[...]).astype(
                out_ref.dtype
            )
        for t in range(n_shard):
            out_ref[0, t, PIECES - 1] = matmul(proj_ref[0, 0], act_ref[t]).astype(out_ref.dtype)

    shape = (n_dp, n_shard, PIECES, unit, width)
    return pl.pallas_call(
        kernel,
        grid=(n_dp,),
        in_specs=[per_dp(fc_units), per_dp(proj_units), whole(fc_rows), whole(act_parts)],
        out_specs=pl.BlockSpec((1,) + shape[1:], lambda d: (d, 0, 0, 0, 0)),
        out_shape=jax.ShapeDtypeStruct(shape, jnp.bfloat16),
        compiler_params=pltpu.CompilerParams(vmem_limit_bytes=40 * 1024 * 1024),
        cost_estimate=pl.CostEstimate(
            flops=2 * 8 * n_dp * unit * width * rows,
            bytes_accessed=2 * math.prod(shape),
            transcendentals=0,
        ),
    )(fc_units, proj_units, fc_rows, act_parts)


def early_grads(partial, qkv_units, out_units, qkv_rows, out_rows):
    n_dp, n_shard, _, unit, width = partial.shape
    lefts = jnp.concatenate([qkv_units, out_units], axis=1)
    rights = jnp.stack([qkv_rows, out_rows])
    rows = qkv_rows.shape[0]

    def kernel(partial_ref, left_ref, right_ref, out_ref):
        last = pl.program_id(1) == 1
        out_ref[0, 0, 0] = matmul(left_ref[0, 0], right_ref[0]).astype(out_ref.dtype)

        @pl.when(last)
        def _():
            out_ref[0, 0, 1] = matmul(left_ref[0, 1], right_ref[1]).astype(out_ref.dtype)

        @pl.when(jnp.logical_not(last))
        def _():
            out_ref[0, 0, 1] = matmul(left_ref[0, 1], right_ref[0]).astype(out_ref.dtype)

    return pl.pallas_call(
        kernel,
        grid=(n_dp, 2),
        in_specs=[
            pl.BlockSpec(memory_space=pl.ANY),
            pl.BlockSpec((1, 2, unit, rows), lambda d, j: (d, j, 0, 0)),
            pl.BlockSpec(rights.shape, lambda d, j: (0, 0, 0)),
        ],
        out_specs=pl.BlockSpec((1, 1, 2, unit, width), lambda d, j: (d, j, 0, 0, 0)),
        out_shape=jax.ShapeDtypeStruct(partial.shape, partial.dtype),
        input_output_aliases={0: 0},
        compiler_params=pltpu.CompilerParams(vmem_limit_bytes=40 * 1024 * 1024),
        cost_estimate=pl.CostEstimate(
            flops=2 * 4 * n_dp * unit * width * rows,
            bytes_accessed=2 * 4 * n_dp * unit * width,
            transcendentals=0,
        ),
    )(partial, lefts, rights)


def fits(w_qkv, w_attn_out, w_fc, w_proj, n_dp, n_shard):
    unit = w_proj.shape[1]
    return (
        n_shard == 4
        and n_dp % COLS == 0
        and n_dp > COLS
        and unit % 8 == 0
        and w_qkv.shape[1] == 3 * unit
        and w_attn_out.shape[1] == unit
        and w_fc.shape[1] == 4 * unit
        and w_proj.shape[0] == w_qkv.shape[0] * n_shard
    )


def on_device(
    tokens_in,
    cotangent,
    segment_ids,
    w_qkv,
    w_attn_out,
    w_fc,
    w_proj,
    small_w,
    moment_qkv,
    moment_attn_out,
    moment_fc,
    moment_proj,
    moment_small,
    second_qkv,
    second_attn_out,
    second_fc,
    second_proj,
    second_small,
):
    n_dp = lax.axis_size("dp")
    n_shard = lax.axis_size("shard")
    if not fits(w_qkv, w_attn_out, w_fc, w_proj, n_dp, n_shard):
        return on_device_general(
            tokens_in,
            cotangent,
            segment_ids,
            w_qkv,
            w_attn_out,
            w_fc,
            w_proj,
            small_w,
            moment_qkv,
            moment_attn_out,
            moment_fc,
            moment_proj,
            moment_small,
            second_qkv,
            second_attn_out,
            second_fc,
            second_proj,
            second_small,
        )
    rows_own = w_qkv.shape[0]
    cols_qkv, cols_out = w_qkv.shape[1], w_attn_out.shape[1]
    unit = w_proj.shape[1]
    small_count = small_w.shape[0]
    cut = jnp.concatenate(
        [w.astype(jnp.bfloat16).T for w in (w_qkv, w_attn_out, w_fc)], axis=0
    ).reshape(n_shard, PIECES - 1, unit, rows_own)
    gathered, small_all = gather_rows(
        cut,
        w_proj.astype(jnp.bfloat16).T,
        pad_rows(small_w.astype(jnp.bfloat16), eight(small_count)),
        n_dp,
        n_shard,
    )

    def by_unit(rows_in):
        return rows_in.T.reshape(n_dp, -1, unit, rows_in.shape[0])

    small_vals = jnp.swapaxes(small_all, 0, 1).reshape(-1, D)[:small_count].astype(jnp.float32)
    gain_one = small_vals[0]
    shift_one = small_vals[1]
    q_bias = small_vals[2]
    v_bias = small_vals[3]
    out_bias = small_vals[4]
    gain_two = small_vals[5]
    shift_two = small_vals[6]
    fc_bias = small_vals[7:11].reshape(FF)
    proj_bias = small_vals[11]
    tok_rows = tokens_in.shape[0]
    group_size = segment_ids.shape[0]
    shard_index = lax.axis_index("shard")
    own_seg = lax.dynamic_slice_in_dim(segment_ids, shard_index * tok_rows, tok_rows)
    query_pos = shard_index * tok_rows + jnp.arange(tok_rows, dtype=jnp.int32)
    x_rows = tokens_in.astype(jnp.float32)
    normed_one, inv_one, ln_one = norm_forward(x_rows, gain_one, shift_one)
    ln_one_half = ln_one.astype(jnp.bfloat16)
    qkv_rows = forward_product(ln_one_half, gathered, QKV_BLOCKS) + jnp.concatenate(
        [q_bias, jnp.zeros_like(q_bias), v_bias]
    )
    queries = qkv_rows[:, :D].astype(jnp.bfloat16)
    kv_half = qkv_rows[:, D:].astype(jnp.bfloat16)
    kv_all = lax.all_gather(kv_half, "shard", axis=0, tiled=True)
    key_all = kv_all[:, :D]
    value_all = kv_all[:, D:]
    key_pos = jnp.arange(group_size, dtype=jnp.int32)
    allowed = (
        (own_seg[:, None] == segment_ids[None, :])
        & (key_pos[None, :] <= query_pos[:, None])
        & ((own_seg >= 0)[:, None] | (key_pos[None, :] == query_pos[:, None]))
    )
    attended, log_total = attend_forward(queries, key_all, value_all, allowed)
    resid = x_rows + forward_product(attended, gathered, OUT_BLOCKS) + out_bias
    normed_two, inv_two, ln_two = norm_forward(resid, gain_two, shift_two)
    ln_two_half = ln_two.astype(jnp.bfloat16)
    pre_act = forward_product(ln_two_half, gathered, FC_BLOCKS) + fc_bias
    act_half = jax.nn.gelu(pre_act, approximate=False).astype(jnp.bfloat16)
    act_parts = jnp.stack([act_half[:, t * D : (t + 1) * D] for t in range(n_shard)])
    out_act = (resid + forward_product(act_parts, gathered, PROJ_BLOCKS) + proj_bias).astype(
        jnp.bfloat16
    )
    valid = (own_seg >= 0).astype(jnp.float32)
    grad_z = cotangent.astype(jnp.float32) * valid[:, None]
    gz_half = grad_z.astype(jnp.bfloat16)
    gz_units = by_unit(gz_half)
    d_act = backward_product(gz_units, gathered, PROJ_BLOCKS)
    d_pre = jnp.concatenate(list(d_act), axis=1) * gelu_slope(pre_act)
    gu_half = d_pre.astype(jnp.bfloat16)
    gu_units = by_unit(gu_half)
    d_ln_two = backward_product(gu_units, gathered, FC_BLOCKS)
    d_resid = grad_z + norm_backward(d_ln_two, normed_two, inv_two, gain_two)
    gh_half = d_resid.astype(jnp.bfloat16)
    gh_units = by_unit(gh_half)
    grad_attn = backward_product(gh_units, gathered, OUT_BLOCKS).astype(jnp.bfloat16)
    d_query, d_keys_all, d_values_all = attend_backward(
        queries, key_all, value_all, allowed, log_total, attended, grad_attn
    )
    d_kv = lax.psum_scatter(
        jnp.concatenate(
            [d_keys_all.astype(jnp.bfloat16), d_values_all.astype(jnp.bfloat16)], axis=1
        ),
        "shard",
        scatter_dimension=0,
        tiled=True,
    )
    d_values = d_kv[:, D:].astype(jnp.float32)
    gqkv_half = jnp.concatenate([d_query.astype(jnp.bfloat16), d_kv], axis=1)
    gqkv_units = by_unit(gqkv_half)
    d_ln_one = backward_product(gqkv_units, gathered, QKV_BLOCKS)
    grad_input = (d_resid + norm_backward(d_ln_one, normed_one, inv_one, gain_one)).astype(
        jnp.bfloat16
    )
    small_rows = jnp.stack(
        [
            jnp.sum(d_ln_one * normed_one, axis=0),
            jnp.sum(d_ln_one, axis=0),
            jnp.sum(d_query, axis=0),
            jnp.sum(d_values, axis=0),
            jnp.sum(d_resid, axis=0),
            jnp.sum(d_ln_two * normed_two, axis=0),
            jnp.sum(d_ln_two, axis=0),
        ]
    )
    small_grad = jnp.concatenate(
        [small_rows, jnp.sum(d_pre, axis=0).reshape(4, D), jnp.sum(grad_z, axis=0)[None]], axis=0
    )
    small_send = jnp.swapaxes(
        pad_rows(small_grad.astype(jnp.bfloat16).astype(jnp.float32), eight(small_count)).reshape(
            -1, n_shard, rows_own
        ),
        0,
        1,
    )

    late = late_grads(gu_units, gz_units, ln_two_half, act_parts, n_shard)
    grads = early_grads(late, gqkv_units, gh_units, ln_one_half, attended)
    swapped, proj_sum, small_sum = reduce_rows(grads, small_send, n_dp, n_shard)
    mixed_sum = swapped.reshape(-1, rows_own).astype(jnp.float32)
    grad_qkv = mixed_sum[:cols_qkv].T
    grad_attn_out = mixed_sum[cols_qkv : cols_qkv + cols_out].T
    grad_fc = mixed_sum[cols_qkv + cols_out :].T
    grad_proj = proj_sum.astype(jnp.float32).T
    grad_small = small_sum[:small_count]
    upd_qkv = adam_update(w_qkv, moment_qkv, second_qkv, grad_qkv, WEIGHT_DECAY)
    upd_out = adam_update(w_attn_out, moment_attn_out, second_attn_out, grad_attn_out, WEIGHT_DECAY)
    upd_fc = adam_update(w_fc, moment_fc, second_fc, grad_fc, WEIGHT_DECAY)
    upd_proj = adam_update(w_proj, moment_proj, second_proj, grad_proj, WEIGHT_DECAY)
    upd_small = adam_update(small_w, moment_small, second_small, grad_small, 0.0)
    return (
        out_act,
        grad_input,
        grad_qkv,
        grad_attn_out,
        grad_fc,
        grad_proj,
        grad_small,
        upd_qkv[0],
        upd_out[0],
        upd_fc[0],
        upd_proj[0],
        upd_small[0],
        upd_qkv[1],
        upd_out[1],
        upd_fc[1],
        upd_proj[1],
        upd_small[1],
        upd_qkv[2],
        upd_out[2],
        upd_fc[2],
        upd_proj[2],
        upd_small[2],
    )


def solution(mesh):
    return jax.shard_map(
        on_device,
        mesh=mesh,
        in_specs=(
            P(("dp", "shard"), None),
            P(("dp", "shard"), None),
            P("dp"),
            P("shard", "dp"),
            P("shard", "dp"),
            P("shard", "dp"),
            P("shard", "dp"),
            P(None, "shard"),
            P("shard", "dp"),
            P("shard", "dp"),
            P("shard", "dp"),
            P("shard", "dp"),
            P(None, "shard"),
            P("shard", "dp"),
            P("shard", "dp"),
            P("shard", "dp"),
            P("shard", "dp"),
            P(None, "shard"),
        ),
        out_specs=(
            P(("dp", "shard"), None),
            P(("dp", "shard"), None),
            P("shard", "dp"),
            P("shard", "dp"),
            P("shard", "dp"),
            P("shard", "dp"),
            P(None, "shard"),
            P("shard", "dp"),
            P("shard", "dp"),
            P("shard", "dp"),
            P("shard", "dp"),
            P(None, "shard"),
            P("shard", "dp"),
            P("shard", "dp"),
            P("shard", "dp"),
            P("shard", "dp"),
            P(None, "shard"),
            P("shard", "dp"),
            P("shard", "dp"),
            P("shard", "dp"),
            P("shard", "dp"),
            P(None, "shard"),
        ),
        check_vma=False,
    )
```
